32 devices in a mesh: groups: 2 (over x), rows: 8 (over z, y), cols: 2 (over core).
Axes of the slice: x: 2, y: 2, z: 4, core: 2. Of those that a mesh axis runs over, the one named last changes fastest.
Arguments:
- depth: float32 [4096, 512], P(('groups', 'rows'), 'cols'), parts along dimension 0, may hold values from 0 to 1.5, as said below
- velocity: float32 [2, 4096, 512], P(None, ('groups', 'rows'), 'cols'), parts along dimension 1, may hold values from -1 to 1
- bed: float32 [4096, 512], P(('groups', 'rows'), 'cols'), parts along dimension 0, may hold values from 0 to 0.5
- slots: int32 [16, 2, 3], P(('groups', 'rows'), 'cols'), parts along dimension 0, may hold values from -1 to 63, as said below
Outputs:
- packed: float32 [16, 2, 3, 3, 128, 128], P(('groups', 'rows'), 'cols'), parts along dimension 0
The draws below stay inside these ranges and needn't reach their ends.
There are 2 independent parts, one for each index of `groups`. The reference program is written for one: setup_inputs(seed, part) draws one part's arguments, and reference() takes and returns one part's arrays. A program takes and returns all parts, laid end to end along the dimension named above; each array names one. Nothing has to cross between parts.
Inputs may be any that keep to these rules, and one draw needn't show every extreme that they name: Each non-negative entry of slots[r, c] is the id of a tile of device (r, c)'s own block (tile rows r * 2 to r * 2 + 1, tile columns c * 2 to c * 2 + 1) or of the block of its partner, device ((r + 4) mod 8, c). No id is listed twice. Every device's partner lists at least one and at most 2 tiles of that device's block, and some device's partner lists exactly 2; at most 3 entries of one list are ids, and some list has exactly 3. `depth`: depth is zero on every cell of a tile that no slot list names.
All inputs are finite; a program needn't handle non-finite values.
Results may differ from the reference program's by a relative error of at most 0.0003.
Values sent between devices are 32-bit elements; how exact they have to be, the bound alone decides.
No kernel may reach another device: no remote copies, remote signals or barrier semaphores. Data moves between devices by JAX's collectives and lax.ppermute only.
A program may use at most 64 MiB of HBM per device.

```python
import jax
import jax.numpy as jnp

TILE = 128
RT = 2
CT = 2
SLOTS = 3
GRID_ROWS = 2048
GRID_COLS = 512
N_ROWS = 8
N_COLS = 2


def tile_layout(key):
    half = N_ROWS // 2
    per_device = RT * CT
    pair_count = half * N_COLS
    keys = jax.random.split(key, 6)
    heavy_wet = jax.random.randint(keys[0], (pair_count,), per_device // 2, per_device + 1)
    light_wet = jax.random.randint(keys[1], (pair_count,), 1, per_device // 2 + 1)
    first_pair = jax.random.randint(keys[2], (), 0, pair_count)
    second_pair = (first_pair + 1 + jax.random.randint(keys[3], (), 0, pair_count - 1)) % pair_count
    pair_ids = jnp.arange(pair_count)
    heavy_wet = jnp.where(pair_ids == first_pair, per_device, heavy_wet)
    light_wet = jnp.where(pair_ids == first_pair, 1, light_wet)
    heavy_wet = jnp.where(pair_ids == second_pair, per_device, heavy_wet)
    light_wet = jnp.where(pair_ids == second_pair, per_device // 2, light_wet)
    top_heavy = jax.random.randint(keys[4], (pair_count,), 0, 2)
    heavy_send = (heavy_wet - light_wet) // 2 + 1
    light_send = jnp.ones_like(heavy_send)
    top_wet = jnp.where(top_heavy == 1, heavy_wet, light_wet)
    bottom_wet = jnp.where(top_heavy == 1, light_wet, heavy_wet)
    top_send = jnp.where(top_heavy == 1, heavy_send, light_send)
    bottom_send = jnp.where(top_heavy == 1, light_send, heavy_send)
    wet_count = jnp.concatenate([top_wet.reshape(half, N_COLS), bottom_wet.reshape(half, N_COLS)], axis=0)
    sent_count = jnp.concatenate([top_send.reshape(half, N_COLS), bottom_send.reshape(half, N_COLS)], axis=0)
    scores = jax.random.randint(keys[5], (N_ROWS, N_COLS, per_device), 0, 2 ** 20) * per_device + jnp.arange(per_device)
    order = jnp.argsort(scores, axis=-1)
    ranks = jnp.argsort(order, axis=-1)
    wet = ranks < wet_count[..., None]
    position = jnp.cumsum(wet.astype(jnp.int32), axis=-1) - 1
    sent = wet & (position >= (wet_count - sent_count)[..., None])
    return (wet, sent)


def draw_slots(key, part):
    wet, sent = tile_layout(jax.random.fold_in(key, 7))
    per_device = RT * CT
    half = N_ROWS // 2
    tile_cols_all = CT * N_COLS
    row_ids = jnp.arange(N_ROWS)[:, None, None]
    col_ids = jnp.arange(N_COLS)[None, :, None]
    local = jnp.arange(per_device)[None, None, :]
    global_ids = (row_ids * RT + local // CT) * tile_cols_all + col_ids * CT + local % CT
    kept = wet & jnp.logical_not(sent)
    taken = jnp.roll(sent, half, axis=0)
    taken_ids = jnp.roll(global_ids, half, axis=0)
    candidate_ids = jnp.concatenate([global_ids, taken_ids], axis=-1)
    candidate_flags = jnp.concatenate([kept, taken], axis=-1).astype(jnp.int32)
    target = jnp.cumsum(candidate_flags, axis=-1) - 1
    target = jnp.where(candidate_flags == 1, target, SLOTS)
    hits = (target[..., :, None] == jnp.arange(SLOTS)[None, None, None, :]).astype(jnp.int32)
    return (jnp.sum(hits * (candidate_ids + 1)[..., None], axis=-2) - 1).astype(jnp.int32)


def draw_depth(key, part):
    wet, sent = tile_layout(jax.random.fold_in(key, 7))
    tiles = wet.reshape(N_ROWS, N_COLS, RT, CT).transpose(0, 2, 1, 3).reshape(N_ROWS * RT, N_COLS * CT).astype(jnp.float32)
    base_key, cell_key = jax.random.split(jax.random.fold_in(key, 11))
    cell_shape = (N_ROWS * RT * TILE, N_COLS * CT * TILE)
    base = jax.random.uniform(base_key, tiles.shape, jnp.float32, 0.2, 1.0)
    rough = jax.random.uniform(cell_key, cell_shape, jnp.float32, -0.4, 0.5)
    base_cells = jnp.repeat(jnp.repeat(base, TILE, axis=0), TILE, axis=1)
    wet_cells = jnp.repeat(jnp.repeat(tiles, TILE, axis=0), TILE, axis=1)
    return (wet_cells * jnp.maximum(0.0, base_cells + rough)).astype(jnp.float32)


def level_of(rng, dims, shards, smallest, high):
    gain, own = 1.0, jax.random.fold_in(rng, 6)
    for dim, parts in shards:
        heights = jnp.exp(jax.random.uniform(jax.random.fold_in(own, dim), (parts,), jnp.float32, smallest / len(shards), high / len(shards)))
        gain = gain * jnp.repeat(heights, dims[dim] // parts).reshape([-1 if axis == dim else 1 for axis in range(len(dims))])
    return gain


def setup_inputs(seed: int = 0, part: int = 0) -> dict:
    seeds = jax.random.split(jax.random.key(seed), 5)
    part_keys = jax.random.split(jax.random.fold_in(seeds[4], part), 5)
    return {
        "depth": draw_depth(jax.random.fold_in(jax.random.fold_in(seeds[4], part), 71), part),
        "velocity": jnp.clip(jax.random.uniform(part_keys[1], (2, GRID_ROWS, GRID_COLS), jnp.float32, -1.0, 1.0) * level_of(part_keys[1], (2, GRID_ROWS, GRID_COLS), ((1, 8), (2, 2)), -0.4, 0.0), -1.0, 1.0),
        "bed": jnp.clip(0.5 * jax.random.uniform(part_keys[2], (GRID_ROWS, GRID_COLS), jnp.float32) ** level_of(part_keys[2], (GRID_ROWS, GRID_COLS), ((0, 8), (1, 2)), -0.2, 0.2), 0.0, 0.5),
        "slots": draw_slots(jax.random.fold_in(jax.random.fold_in(seeds[4], part), 71), part),
    }


GRAVITY = 9.81
TIME_STEP = 0.04
DRY_DEPTH = 0.05
SPEED_FLOOR = 0.5

def take_range(values, lower_end, upper_end, direction):
    selector = [slice(None)] * values.ndim
    selector[direction] = slice(lower_end, upper_end)
    return values[tuple(selector)]

def minmod(left_diff, right_diff):
    return 0.5 * (jnp.sign(left_diff) + jnp.sign(right_diff)) * jnp.minimum(jnp.abs(left_diff), jnp.abs(right_diff))

def face_values(values, direction):
    change = take_range(values, 1, None, direction) - take_range(values, 0, -1, direction)
    slope = minmod(take_range(change, 0, -1, direction), take_range(change, 1, None, direction))
    middle = take_range(values, 1, -1, direction)
    return (middle - 0.5 * slope, middle + 0.5 * slope)

def velocity_from(water, flow):
    return 2.0 * water * flow / (water * water + jnp.maximum(water * water, DRY_DEPTH * DRY_DEPTH))

def flux_sweep(water, normal, across, ground, direction):
    water_low, water_high = face_values(water, direction)
    normal_low, normal_high = face_values(normal, direction)
    across_low, across_high = face_values(across, direction)
    ground_low, ground_high = face_values(ground, direction)

    def left_side(values):
        return take_range(values, 0, -1, direction)

    def right_side(values):
        return take_range(values, 1, None, direction)
    water_left = left_side(water_high)
    water_right = right_side(water_low)
    speed_left = velocity_from(water_left, left_side(normal_high))
    speed_right = velocity_from(water_right, right_side(normal_low))
    drift_left = velocity_from(water_left, left_side(across_high))
    drift_right = velocity_from(water_right, right_side(across_low))
    ground_left = left_side(ground_high)
    ground_right = right_side(ground_low)
    ground_top = jnp.maximum(ground_left, ground_right)
    level_left = jnp.maximum(0.0, water_left + ground_left - ground_top)
    level_right = jnp.maximum(0.0, water_right + ground_right - ground_top)
    wave_left = jnp.sqrt(GRAVITY * level_left)
    wave_right = jnp.sqrt(GRAVITY * level_right)
    lower_speed = jnp.minimum(jnp.minimum(speed_left - wave_left, speed_right - wave_right), 0.0)
    upper_speed = jnp.maximum(jnp.maximum(speed_left + wave_left, speed_right + wave_right), 0.0)
    spread = jnp.maximum(upper_speed - lower_speed, SPEED_FLOOR)

    def riemann_flux(flux_left, flux_right, kept_left, kept_right):
        return (upper_speed * flux_left - lower_speed * flux_right + upper_speed * lower_speed * (kept_right - kept_left)) / spread
    mass_left = level_left * speed_left
    mass_right = level_right * speed_right
    mass_flux = riemann_flux(mass_left, mass_right, level_left, level_right)
    push_flux = riemann_flux(mass_left * speed_left + 0.5 * GRAVITY * level_left * level_left, mass_right * speed_right + 0.5 * GRAVITY * level_right * level_right, mass_left, mass_right)
    side_flux = riemann_flux(mass_left * drift_left, mass_right * drift_right, level_left * drift_left, level_right * drift_right)

    def lower_face(values):
        return take_range(values, 0, -1, direction)

    def upper_face(values):
        return take_range(values, 1, None, direction)
    cell_low = take_range(water_low, 1, -1, direction)
    cell_high = take_range(water_high, 1, -1, direction)
    ground_cell_low = take_range(ground_low, 1, -1, direction)
    ground_cell_high = take_range(ground_high, 1, -1, direction)
    below_level = lower_face(level_right)
    above_level = upper_face(level_left)
    mass_rate = lower_face(mass_flux) - upper_face(mass_flux)
    push_rate = lower_face(push_flux) - upper_face(push_flux) + 0.5 * GRAVITY * (cell_low * cell_low - below_level * below_level) - 0.5 * GRAVITY * (cell_high * cell_high - above_level * above_level) + 0.5 * GRAVITY * (cell_low + cell_high) * (ground_cell_low - ground_cell_high)
    side_rate = lower_face(side_flux) - upper_face(side_flux)
    return (mass_rate, push_rate, side_rate)

def advance(state, statics):
    water = state[..., 0, :, :]
    flow_x = state[..., 1, :, :]
    flow_y = state[..., 2, :, :]
    ground = statics[..., 0, :, :]
    active = statics[..., 1, :, :]

    def rows_inner(values):
        return values[..., 2:-2, :]

    def cols_inner(values):
        return values[..., :, 2:-2]

    def center(values):
        return values[..., 2:-2, 2:-2]
    mass_x, push_x, side_x = flux_sweep(rows_inner(water), rows_inner(flow_x), rows_inner(flow_y), rows_inner(ground), -1)
    mass_y, push_y, side_y = flux_sweep(cols_inner(water), cols_inner(flow_y), cols_inner(flow_x), cols_inner(ground), -2)
    new_water = center(water) + TIME_STEP * (mass_x + mass_y)
    new_flow_x = center(flow_x) + TIME_STEP * (push_x + side_y)
    new_flow_y = center(flow_y) + TIME_STEP * (side_x + push_y)
    updated = jnp.stack([new_water, new_flow_x, new_flow_y], axis=-3)
    keeping = center(active)[..., None, :, :] > 0.5
    return jnp.where(keeping, updated, center(state))

def reference(depth, velocity, bed, slots):
    state = jnp.stack([depth, depth * velocity[0], depth * velocity[1]])
    tile_rows = depth.shape[0] // TILE
    tile_cols = depth.shape[1] // TILE
    tile_total = tile_rows * tile_cols
    listed = slots.reshape(-1)
    targets = jnp.where(listed >= 0, listed, tile_total).astype(jnp.int32)
    flags = jnp.zeros((tile_total + 1,), jnp.float32).at[targets].set(1.0)[:tile_total]
    active_tiles = flags.reshape(tile_rows, tile_cols)
    active_cells = jnp.repeat(jnp.repeat(active_tiles, TILE, axis=0), TILE, axis=1)
    statics = jnp.pad(jnp.stack([bed, active_cells]), ((0, 0), (2, 2), (2, 2)))
    for sweep_index in range(2):
        state = advance(jnp.pad(state, ((0, 0), (2, 2), (2, 2))), statics)
    tiles = state.reshape(3, tile_rows, TILE, tile_cols, TILE).transpose(1, 3, 0, 2, 4).reshape(tile_total, 3, TILE, TILE)
    chosen = tiles[jnp.maximum(listed, 0).astype(jnp.int32)] * (listed >= 0).astype(jnp.float32)[:, None, None, None]
    return chosen.reshape(slots.shape + (3, TILE, TILE))
```

```python
import jax
import jax.numpy as jnp
from jax import lax
from jax.experimental import pallas as pl
from jax.experimental.pallas import tpu as pltpu
from jax.sharding import PartitionSpec as P

TILE = 128
RT = 2
CT = 2
SLOTS = 3
MOVED = RT * CT // 2
ROWS = RT * TILE
COLS = CT * TILE
PAD = 16
DEEP = ROWS + 2 * PAD
SEAM = 24
SEAM_DEEP = SEAM + 2 * PAD
REACH = 4

GRAVITY = 9.81
TIME_STEP = 0.04
DRY_DEPTH = 0.05
SPEED_FLOOR = 0.5
ROOT_GRAVITY = GRAVITY**0.5
TINY = 1.2e-38

VMEM = pl.BlockSpec(memory_space=pltpu.VMEM)
SMEM = pl.BlockSpec(memory_space=pltpu.SMEM)


def f32(*shape):
    return jax.ShapeDtypeStruct(shape, jnp.float32)


def call(kernel, name, ins, outs, scratch=(), **extra):
    return pl.pallas_call(
        kernel,
        name=name,
        in_specs=list(ins),
        out_specs=tuple(VMEM for _ in outs),
        out_shape=tuple(outs),
        scratch_shapes=list(scratch),
        compiler_params=pltpu.CompilerParams(vmem_limit_bytes=20 * 2**20),
        **extra,
    )


def limited(down, up):
    return 0.5 * jnp.maximum(jnp.minimum(down, jnp.maximum(up, 0.0)), jnp.minimum(up, 0.0))


def speeds(water, normal, across):
    square = water * water
    factor = (water + water) / (square + jnp.maximum(square, DRY_DEPTH * DRY_DEPTH))
    return factor * normal, factor * across


def wave_speed(level):
    return (ROOT_GRAVITY * level) * lax.rsqrt(jnp.maximum(level, TINY))


def face_flux(left, right):
    water_l, speed_l, drift_l, ground_l = left
    water_r, speed_r, drift_r, ground_r = right
    top = jnp.maximum(ground_l, ground_r)
    level_l = jnp.maximum(water_l + (ground_l - top), 0.0)
    level_r = jnp.maximum(water_r + (ground_r - top), 0.0)
    wave_l = wave_speed(level_l)
    wave_r = wave_speed(level_r)
    lower = jnp.minimum(jnp.minimum(speed_l - wave_l, speed_r - wave_r), 0.0)
    upper = jnp.maximum(jnp.maximum(speed_l + wave_l, speed_r + wave_r), 0.0)
    inverse = 1.0 / jnp.maximum(upper - lower, SPEED_FLOOR)
    up = upper * inverse
    low = lower * inverse
    both = upper * low
    part_l = level_l * (up * speed_l - both)
    part_r = level_r * (both - low * speed_r)
    press_l = (0.5 * GRAVITY) * (level_l * level_l)
    press_r = (0.5 * GRAVITY) * (level_r * level_r)
    mass = part_l + part_r
    push = part_l * speed_l + part_r * speed_r + up * press_l - low * press_r
    side = part_l * drift_l + part_r * drift_r
    return mass, push - press_l, push - press_r, side


def sweep(src, dst, width, steps, src_row, dst_row, lane_flow, row_flow):
    lane = lax.broadcasted_iota(jnp.int32, (8, 128), 1)
    sub = lax.broadcasted_iota(jnp.int32, (8, 128), 0)
    cols = range(width)

    def from_lower(values):
        turned = [pltpu.roll(v, 1, 1) for v in values]
        return [jnp.where(lane == 0, turned[w - 1], turned[w]) for w in cols]

    def from_upper(values):
        turned = [pltpu.roll(v, 127, 1) for v in values]
        return [jnp.where(lane == 127, turned[(w + 1) % width], turned[w]) for w in cols]

    def step(i, carry):
        shift = pl.multiple_of(i * 8, 8)
        row = shift + src_row
        x = [[src[f, w, pl.ds(row, 8), :] for w in cols] for f in range(4)]
        low, high, half = [], [], []
        for f in (0, lane_flow, row_flow, 3):
            before = from_lower(x[f])
            down = [x[f][w] - before[w] for w in cols]
            up = from_upper(down)
            hs = [limited(down[w], up[w]) for w in cols]
            low.append([x[f][w] - hs[w] for w in cols])
            high.append([x[f][w] + hs[w] for w in cols])
            half.append(hs)
        fast = [speeds(high[0][w], high[1][w], high[2][w]) for w in cols]
        slow = [speeds(low[0][w], low[1][w], low[2][w]) for w in cols]
        left = [
            from_lower(high[0]),
            from_lower([v[0] for v in fast]),
            from_lower([v[1] for v in fast]),
            from_lower(high[3]),
        ]
        flux = [
            face_flux([left[k][w] for k in range(4)], (low[0][w], slow[w][0], slow[w][1], low[3][w]))
            for w in cols
        ]
        mass_up = from_upper([v[0] for v in flux])
        push_up = from_upper([v[1] for v in flux])
        side_up = from_upper([v[3] for v in flux])
        now = []
        for w in cols:
            weight = (2.0 * GRAVITY) * x[0][w]
            gain_water = flux[w][0] - mass_up[w]
            gain_lane = flux[w][2] - push_up[w] - weight * (half[0][w] + half[3][w])
            gain_row = flux[w][3] - side_up[w]
            low_r, high_r, half_r = [], [], []
            for f in (0, row_flow, lane_flow, 3):
                before = src[f, w, pl.ds(row - 1, 8), :]
                after = src[f, w, pl.ds(row + 1, 8), :]
                hs = limited(x[f][w] - before, after - x[f][w])
                low_r.append(x[f][w] - hs)
                high_r.append(x[f][w] + hs)
                half_r.append(hs)
            fast_n, fast_t = speeds(high_r[0], high_r[1], high_r[2])
            slow_n, slow_t = speeds(low_r[0], low_r[1], low_r[2])
            old_high, old_flux, old_gain = carry[w]
            high_now = tuple(pltpu.roll(v, 1, 0) for v in (high_r[0], fast_n, fast_t, high_r[3]))
            left_r = [jnp.where(sub == 0, o, n) for o, n in zip(old_high, high_now)]
            mass, push_l, push_r, side = face_flux(left_r, (low_r[0], slow_n, slow_t, low_r[3]))
            gain = (
                gain_water + mass,
                gain_lane + side,
                gain_row + push_r - weight * (half_r[0] + half_r[3]),
            )
            flux_now = tuple(pltpu.roll(v, 7, 0) for v in (mass, side, push_l))
            out = shift + (dst_row - 8)
            for f, g, o, n in zip((0, lane_flow, row_flow), old_gain, old_flux, flux_now):
                kept = src[f, w, pl.ds(row - 8, 8), :]
                dst[f, w, pl.ds(out, 8), :] = kept + TIME_STEP * (g - jnp.where(sub == 7, n, o))
            now.append((high_now, flux_now, gain))
        return tuple(now)

    zero = jnp.zeros((8, 128), jnp.float32)
    start = tuple(((zero,) * 4, (zero,) * 3, (zero,) * 3) for _ in cols)
    lax.fori_loop(0, steps, step, start)


def load_kernel(depth, velocity, bed, state, moved):
    blank = jnp.zeros((8, TILE), jnp.float32)
    for w in range(CT):
        cols = slice(w * TILE, (w + 1) * TILE)
        for f in range(4):
            for r in (0, 8, PAD + ROWS, PAD + ROWS + 8):
                state[f, w, r : r + 8, :] = blank
                moved[f, w, r : r + 8, :] = blank
        for r in range(0, ROWS, 8):
            rows = slice(r, r + 8)
            held = slice(PAD + r, PAD + r + 8)
            water = depth[rows, cols]
            ground = bed[rows, cols]
            state[0, w, held, :] = water
            state[1, w, held, :] = water * velocity[0, rows, cols]
            state[2, w, held, :] = water * velocity[1, rows, cols]
            state[3, w, held, :] = ground
            moved[3, w, held, :] = ground
    sweep(state, moved, CT, ROWS // 8 + 1, PAD, PAD, 1, 2)


class Lists:
    def __init__(self, listed, partner):
        self.rows = lax.axis_index("rows")
        self.cols = lax.axis_index("cols")
        self.span = CT * lax.axis_size("cols")
        self.ids = [
            (self.rows * RT + t // CT) * self.span + self.cols * CT + t % CT for t in range(RT * CT)
        ]
        self.listed = [listed[k] for k in range(SLOTS)]
        self.partner = [partner[k] for k in range(SLOTS)]

    def inside(self, entry):
        found = [entry == i for i in self.ids]
        any_found = found[0]
        local = jnp.int32(0)
        for t in range(1, RT * CT):
            any_found = any_found | found[t]
            local = jnp.where(found[t], jnp.int32(t), local)
        return any_found, local

    def active(self, t):
        hit = self.listed[0] == self.ids[t]
        for entry in self.listed[1:] + self.partner:
            hit = hit | (entry == self.ids[t])
        return hit

    def outgoing(self):
        used = [jnp.bool_(False)] * MOVED
        tile = [jnp.int32(0)] * MOVED
        rank = jnp.int32(0)
        for entry in self.partner:
            own, local = self.inside(entry)
            for k in range(MOVED):
                take = own & (rank == k)
                used[k] = used[k] | take
                tile[k] = jnp.where(take, local, tile[k])
            rank = rank + own.astype(jnp.int32)
        return used, tile


def send_kernel(listed, partner, state, guess, moved, outgoing, final):
    lists = Lists(listed, partner)
    for t in range(RT * CT):
        rows = slice(PAD + (t // CT) * TILE, PAD + (t // CT + 1) * TILE)

        @pl.when(lists.active(t))
        def _(t=t, rows=rows):
            for f in range(3):
                moved[f, t % CT, rows, :] = guess[f, t % CT, rows, :]

        @pl.when(jnp.logical_not(lists.active(t)))
        def _(t=t, rows=rows):
            for f in range(3):
                moved[f, t % CT, rows, :] = state[f, t % CT, rows, :]

    blank = jnp.zeros((8, TILE), jnp.float32)
    for w in range(CT):
        for f in range(4):
            for r in (0, 8, PAD + ROWS, PAD + ROWS + 8):
                moved[f, w, r : r + 8, :] = blank
        moved[3, w, PAD : PAD + ROWS, :] = state[3, w, PAD : PAD + ROWS, :]
    used, tile = lists.outgoing()
    for r in range(RT):
        needed = jnp.bool_(False)
        for k in range(MOVED):
            needed = needed | (used[k] & (tile[k] // CT == r))

        @pl.when(needed)
        def _(r=r):
            sweep(moved, final.at[r], CT, TILE // 8 + 2, PAD + r * TILE - 8, PAD - 8, 1, 2)

    for k in range(MOVED):
        r = tile[k] // CT
        c = tile[k] % CT
        for f in range(3):
            for b in range(0, TILE, 8):
                outgoing[k, f, b : b + 8, :] = final[r, f, c, PAD + b : PAD + b + 8, :]


def keep_kernel(listed, partner, moved, final):
    lists = Lists(listed, partner)
    used, tile = lists.outgoing()
    for r in range(RT):
        sent = jnp.bool_(False)
        for k in range(MOVED):
            sent = sent | (used[k] & (tile[k] // CT == r))
        own = jnp.bool_(False)
        for entry in lists.listed:
            inside, local = lists.inside(entry)
            own = own | (inside & (local // CT == r))

        @pl.when(own & jnp.logical_not(sent))
        def _(r=r):
            sweep(moved, final.at[r], CT, TILE // 8 + 2, PAD + r * TILE - 8, PAD - 8, 1, 2)


def edge_kernel(listed, partner, state, strips):
    lists = Lists(listed, partner)
    lane = lax.broadcasted_iota(jnp.int32, (TILE, TILE), 1)
    last = slice(PAD + ROWS - 8, PAD + ROWS)
    for f in range(4):
        for w in range(CT):
            cols = slice(w * TILE, (w + 1) * TILE)
            strips[f, 0:8, cols] = state[f, w, last, :]
            strips[f, 8:16, cols] = state[f, w, PAD : PAD + 8, :]
        for r in range(RT):
            rows = slice(PAD + r * TILE, PAD + (r + 1) * TILE)
            ends = jnp.where(lane < TILE // 2, state[f, 0, rows, :], state[f, CT - 1, rows, :])
            turned = ends.T
            cols = slice(r * TILE, (r + 1) * TILE)
            strips[f, 16:24, cols] = turned[TILE - 8 :, :]
            strips[f, 24:32, cols] = turned[:8, :]
    flags = [jnp.where(lists.active(t), 1.0, 0.0) for t in range(RT * CT)]
    for w in range(CT):
        cols = slice(w * TILE, (w + 1) * TILE)
        strips[4, 0:8, cols] = jnp.full((8, TILE), flags[(RT - 1) * CT + w], jnp.float32)
        strips[4, 8:16, cols] = jnp.full((8, TILE), flags[w], jnp.float32)
    for r in range(RT):
        cols = slice(r * TILE, (r + 1) * TILE)
        strips[4, 16:24, cols] = jnp.full((8, TILE), flags[r * CT + CT - 1], jnp.float32)
        strips[4, 24:32, cols] = jnp.full((8, TILE), flags[r * CT], jnp.float32)


def wide_kernel(mine, other, out):
    is_left = lax.axis_index("cols") == 0
    for f in range(5):
        own = jnp.where(is_left, mine[f, 8:12, :], mine[f, 4:8, :])
        near = jnp.where(is_left, other[f, 8:12, :], other[f, 4:8, :])
        out[4 * f : 4 * f + 4, 0:COLS] = jnp.where(is_left, own, near)
        out[4 * f : 4 * f + 4, COLS : 2 * COLS] = jnp.where(is_left, near, own)
    out[20:24, :] = jnp.zeros((4, 2 * COLS), jnp.float32)


def still(dst, src, width):
    for w in range(width):
        rows = slice(PAD, PAD + SEAM)
        alive = src[4, w, rows, :] > 0.5
        for f in range(3):
            dst[f, w, rows, :] = jnp.where(alive, dst[f, w, rows, :], src[f, w, rows, :])


def seam_kernel(listed, partner, mine, other, came, near, fixes, sent, flat, flat2, flat3, tall, tall2, tall3):
    lists = Lists(listed, partner)
    is_left = lists.cols == 0
    lane = lax.broadcasted_iota(jnp.int32, (8, TILE), 1)
    lane4 = lax.broadcasted_iota(jnp.int32, (4, TILE), 1)
    beside = jnp.where(is_left, lane, TILE - 1 - lane) < REACH
    beside4 = jnp.where(is_left, lane4, TILE - 1 - lane4) < REACH
    blank = jnp.zeros((8, TILE), jnp.float32)
    for buffer, width in ((flat, CT + 1), (tall, CT), (flat2, CT + 1), (tall2, CT)):
        for f in range(buffer.shape[0]):
            for w in range(width):
                for r in (0, 8, PAD + SEAM, PAD + SEAM + 8):
                    buffer[f, w, r : r + 8, :] = blank
    for f in range(5):
        for w in range(CT):
            cols = slice(w * TILE, (w + 1) * TILE)
            flat[f, w, PAD : PAD + 8, :] = mine[f, 0:8, cols]
            flat[f, w, PAD + 16 : PAD + 24, :] = mine[f, 8:16, cols]
            tall[f, w, PAD : PAD + 8, :] = mine[f, 16:24, cols]
            tall[f, w, PAD + 16 : PAD + 24, :] = mine[f, 24:32, cols]
            tall[f, w, PAD + 8 : PAD + 12, :] = jnp.where(is_left, other[f, 24:28, cols], 0.0)
            tall[f, w, PAD + 12 : PAD + 16, :] = jnp.where(is_left, 0.0, other[f, 20:24, cols])
        for r, base in ((0, 0), (8, 16)):
            piece = jnp.where(is_left, other[f, r : r + 8, 0:TILE], other[f, r : r + 8, COLS - TILE : COLS])
            flat[f, CT, PAD + base : PAD + base + 8, :] = jnp.where(beside, piece, 0.0)
        rows = slice(4 * f, 4 * f + 4)
        for place, upper in ((8, False), (12, True)):
            halo = jnp.where(is_left == upper, came[rows, :], near[rows, :])
            held = slice(PAD + place, PAD + place + 4)
            for w in range(CT):
                a = halo[:, w * TILE : (w + 1) * TILE]
                b = halo[:, COLS + w * TILE : COLS + (w + 1) * TILE]
                flat[f, w, held, :] = jnp.where(is_left, a, b)
            piece = jnp.where(is_left, halo[:, COLS : COLS + TILE], halo[:, COLS - TILE : COLS])
            flat[f, CT, held, :] = jnp.where(beside4, piece, 0.0)
    for start, middle, end, width, lane_flow, row_flow in (
        (flat, flat2, flat3, CT + 1, 1, 2),
        (tall, tall2, tall3, CT, 2, 1),
    ):
        sweep(start, middle, width, SEAM // 8 + 1, PAD, PAD, lane_flow, row_flow)
        still(middle, start, width)
        for w in range(width):
            middle[3, w, PAD : PAD + SEAM, :] = start[3, w, PAD : PAD + SEAM, :]
        sweep(middle, end, width, SEAM // 8 + 1, PAD, PAD, lane_flow, row_flow)
    for t in range(RT * CT):
        r, c = t // CT, t % CT
        for f in range(3):
            a = PAD + (16 if r == 0 else 4)
            b = PAD + (16 if c == 0 else 4)
            fixes[t, f, 0:4, :] = flat3[f, c, a : a + 4, :]
            fixes[t, f, 4:8, :] = tall3[f, r, b : b + 4, :]
    used, tile = lists.outgoing()
    for k in range(MOVED):
        for f in range(3):
            sent[k, f] = fixes[tile[k], f]


def pack_kernel(listed, partner, early, late, fixes, received, patches, packed, board):
    lists = Lists(listed, partner)
    used, tile = lists.outgoing()
    lane = lax.broadcasted_iota(jnp.int32, (8, TILE), 1)
    sub = lax.broadcasted_iota(jnp.int32, (8, TILE), 0)
    board[...] = jnp.zeros_like(board)
    rank = jnp.int32(0)
    for s in range(SLOTS):
        entry = lists.listed[s]
        own, local = lists.inside(entry)
        foreign = (entry >= 0) & jnp.logical_not(own)
        row = lax.rem(lax.div(jnp.maximum(entry, 0), lists.span), RT)
        col = lax.rem(jnp.maximum(entry, 0), CT)
        swept = jnp.bool_(False)
        for k in range(MOVED):
            swept = swept | (used[k] & (tile[k] // CT == row))
        slot = jnp.minimum(rank, MOVED - 1)
        rank = rank + foreign.astype(jnp.int32)

        def put(cell, fix, s=s, row=row, col=col):
            for f in range(3):
                board[8 * f : 8 * f + 8, :] = fix(f)
            turned = board[...].T
            for f in range(3):
                shift = jnp.where(col == 0, TILE - 8 * f - 4, 2 * TILE - 8 * f - 8)
                shift = lax.rem(shift, TILE)
                strip = fix(f)
                lower = pltpu.roll(strip, 4, 0)
                for b in range(0, TILE, 8):
                    value = cell(f, b)
                    moved = pltpu.roll(turned[b : b + 8, :], shift, 1)
                    edge = jnp.where(col == 0, lane, TILE - 1 - lane) < REACH
                    value = jnp.where(edge, moved, value)
                    if b == 0:
                        value = jnp.where((row == 0) & (sub < REACH), strip, value)
                    if b == TILE - 8:
                        value = jnp.where((row == RT - 1) & (sub >= 8 - REACH), lower, value)
                    packed[s, f, b : b + 8, :] = value

        @pl.when(own & swept)
        def _():
            put(
                lambda f, b: early[row, f, col, PAD + b : PAD + b + 8, :],
                lambda f: fixes[local, f],
            )

        @pl.when(own & jnp.logical_not(swept))
        def _():
            put(
                lambda f, b: late[row, f, col, PAD + b : PAD + b + 8, :],
                lambda f: fixes[local, f],
            )

        @pl.when(foreign)
        def _():
            put(lambda f, b: received[slot, f, b : b + 8, :], lambda f: patches[slot, f])

        @pl.when(entry < 0)
        def _():
            packed[s] = jnp.zeros((3, TILE, TILE), jnp.float32)


def passed_along(block, distance):
    count = lax.axis_size("rows")
    return lax.ppermute(block, "rows", [((i - distance) % count, i) for i in range(count)])


def swapped(block):
    return lax.ppermute(block, "cols", [(0, 1), (1, 0)])


def shards(depth, velocity, bed, slots):
    count = lax.axis_size("rows")
    half = count // 2
    listed = slots[0, 0]
    partner = passed_along(listed, half)
    state, moved = call(
        load_kernel, "load", [VMEM] * 3, [f32(4, CT, DEEP, TILE), f32(4, CT, DEEP, TILE)]
    )(depth, velocity, bed)
    moved, outgoing, early = call(
        send_kernel,
        "send",
        [SMEM, SMEM, VMEM, VMEM],
        [f32(4, CT, DEEP, TILE), f32(MOVED, 3, TILE, TILE), f32(RT, 3, CT, TILE + 2 * PAD, TILE)],
    )(listed, partner, state, moved)
    received = passed_along(outgoing, half)
    (mine,) = call(edge_kernel, "edge", [SMEM, SMEM, VMEM], [f32(5, 32, COLS)])(
        listed, partner, state
    )
    other = swapped(mine)
    (wide,) = call(wide_kernel, "wide", [VMEM, VMEM], [f32(SEAM, 2 * COLS)])(mine, other)
    route = [(2 * r, 2 * r - 1) for r in range(1, count)]
    route += [(2 * r + 1, 2 * r + 2) for r in range(count - 1)]
    came = lax.ppermute(wide, ("rows", "cols"), route)
    near = swapped(came)
    (late,) = call(keep_kernel, "keep", [SMEM, SMEM, VMEM], [f32(RT, 3, CT, TILE + 2 * PAD, TILE)])(
        listed, partner, moved
    )
    flat, tall = (CT + 1, SEAM_DEEP, TILE), (CT, SEAM_DEEP, TILE)
    fixes, sent = call(
        seam_kernel,
        "seam",
        [SMEM, SMEM, VMEM, VMEM, VMEM, VMEM],
        [f32(RT * CT, 3, 8, TILE), f32(MOVED, 3, 8, TILE)],
        [
            pltpu.VMEM((n,) + s, jnp.float32)
            for s in (flat, tall)
            for n in (5, 4, 3)
        ],
    )(listed, partner, mine, other, came, near)
    patches = passed_along(sent, half)
    (packed,) = call(
        pack_kernel,
        "pack",
        [SMEM, SMEM, VMEM, VMEM, VMEM, VMEM, VMEM],
        [f32(SLOTS, 3, TILE, TILE)],
        [pltpu.VMEM((TILE, TILE), jnp.float32)],
    )(listed, partner, early, late, fixes, received, patches)
    return packed[None, None]


def solution(mesh):
    in_specs = (
        P(("groups", "rows"), "cols"),
        P(None, ("groups", "rows"), "cols"),
        P(("groups", "rows"), "cols"),
        P(("groups", "rows"), "cols", None),
    )
    out_specs = P(("groups", "rows"), "cols", None, None, None, None)
    return jax.shard_map(shards, mesh=mesh, in_specs=in_specs, out_specs=out_specs, check_vma=False)
```

```python
import jax
import jax.numpy as jnp
from jax import lax
from jax.experimental import pallas as pl
from jax.experimental.pallas import tpu as pltpu
from jax.sharding import PartitionSpec as P


TILE = 128
RT = 2
CT = 2
SLOTS = 3
MOVED = RT * CT // 2
ROWS = RT * TILE
COLS = CT * TILE
PAD = 16
SEAM = 40
SEAM_DEEP = SEAM + 2 * PAD
SPAN = TILE + 2 * PAD
PART = TILE // 2
REACH = 4
UNROLL_PART = 2
UNROLL_FULL = 3
UNROLL_SEAM = 1

GRAVITY = 9.81
TIME_STEP = 0.04
DRY_DEPTH = 0.05
SPEED_FLOOR = 0.5
ROOT_GRAVITY = GRAVITY**0.5
TINY = 1.2e-38

VMEM = pl.BlockSpec(memory_space=pltpu.VMEM)
HBM = pl.BlockSpec(memory_space=pltpu.HBM)
SMEM = pl.BlockSpec(memory_space=pltpu.SMEM)


def f32(*shape):
    return jax.ShapeDtypeStruct(shape, jnp.float32)


def call(kernel, ins, outs, scratch=(), room=20 * 2**20):
    return pl.pallas_call(
        kernel,
        in_specs=list(ins),
        out_specs=tuple(VMEM for _ in outs),
        out_shape=tuple(outs),
        scratch_shapes=list(scratch),
        compiler_params=pltpu.CompilerParams(vmem_limit_bytes=room),
    )


def limited(down, up):
    return 0.5 * jnp.maximum(jnp.minimum(down, jnp.maximum(up, 0.0)), jnp.minimum(up, 0.0))


def speeds(water, normal, across):
    square = water * water
    factor = (water + water) / (square + jnp.maximum(square, DRY_DEPTH * DRY_DEPTH))
    return factor * normal, factor * across


def wave_speed(level):
    return (ROOT_GRAVITY * level) * lax.rsqrt(jnp.maximum(level, TINY))


def face_flux(left, right):
    water_l, speed_l, drift_l, ground_l = left
    water_r, speed_r, drift_r, ground_r = right
    top = jnp.maximum(ground_l, ground_r)
    level_l = jnp.maximum(water_l + (ground_l - top), 0.0)
    level_r = jnp.maximum(water_r + (ground_r - top), 0.0)
    wave_l = wave_speed(level_l)
    wave_r = wave_speed(level_r)
    lower = jnp.minimum(jnp.minimum(speed_l - wave_l, speed_r - wave_r), 0.0)
    upper = jnp.maximum(jnp.maximum(speed_l + wave_l, speed_r + wave_r), 0.0)
    inverse = 1.0 / jnp.maximum(upper - lower, SPEED_FLOOR)
    up = upper * inverse
    low = lower * inverse
    both = upper * low
    part_l = level_l * (up * speed_l - both)
    part_r = level_r * (both - low * speed_r)
    press_l = (0.5 * GRAVITY) * (level_l * level_l)
    press_r = (0.5 * GRAVITY) * (level_r * level_r)
    mass = part_l + part_r
    push = part_l * speed_l + part_r * speed_r + up * press_l - low * press_r
    side = part_l * drift_l + part_r * drift_r
    return mass, push - press_l, push - press_r, side


def sweep(src, ground, dst, width, steps, row_start, lane_flow, row_flow, unroll, flush):
    sub = lax.broadcasted_iota(jnp.int32, (8, 128), 0)
    cols = range(width)

    def step(i, carry):
        row = row_start + pl.multiple_of(i * 8, 8)

        def read(f, w, offset):
            held = src if f < 3 else ground
            return held[f, w, pl.ds(row + offset, 8), :]

        now = []
        for w in cols:
            x = [read(f, w, 0) for f in range(4)]
            low, high, half = [], [], []
            for f in (0, lane_flow, row_flow, 3):
                down = x[f] - pltpu.roll(x[f], 1, 1)
                hs = limited(down, pltpu.roll(down, TILE - 1, 1))
                low.append(x[f] - hs)
                high.append(x[f] + hs)
                half.append(hs)
            fast = speeds(high[0], high[1], high[2])
            slow = speeds(low[0], low[1], low[2])
            left = [pltpu.roll(v, 1, 1) for v in (high[0], fast[0], fast[1], high[3])]
            mass, push_l, push_r, side = face_flux(left, (low[0], slow[0], slow[1], low[3]))
            weight = (2.0 * GRAVITY) * x[0]
            gain_water = mass - pltpu.roll(mass, TILE - 1, 1)
            gain_lane = push_r - pltpu.roll(push_l, TILE - 1, 1) - weight * (half[0] + half[3])
            gain_row = side - pltpu.roll(side, TILE - 1, 1)
            low, high, half = [], [], []
            for f in (0, row_flow, lane_flow, 3):
                hs = limited(x[f] - read(f, w, -1), read(f, w, 1) - x[f])
                low.append(x[f] - hs)
                high.append(x[f] + hs)
                half.append(hs)
            fast = speeds(high[0], high[1], high[2])
            slow = speeds(low[0], low[1], low[2])
            old_high, old_flux, old_gain = carry[w]
            high_now = tuple(pltpu.roll(v, 1, 0) for v in (high[0], fast[0], fast[1], high[3]))
            left = [jnp.where(sub == 0, o, n) for o, n in zip(old_high, high_now)]
            mass, push_l, push_r, side = face_flux(left, (low[0], slow[0], slow[1], low[3]))
            gain = (
                gain_water + mass,
                gain_lane + side,
                gain_row + push_r - weight * (half[0] + half[3]),
            )
            flux_now = tuple(pltpu.roll(v, 7, 0) for v in (mass, side, push_l))
            for f, g, o, n in zip((0, lane_flow, row_flow), old_gain, old_flux, flux_now):
                dst[f, w, pl.ds(row - 8, 8), :] = read(f, w, -8) + TIME_STEP * (
                    g - jnp.where(sub == 7, n, o)
                )
            now.append((high_now, flux_now, gain))
        return tuple(now)

    zero = jnp.zeros((8, 128), jnp.float32)
    start = tuple(((zero,) * 4, (zero,) * 3, (zero,) * 3) for _ in cols)
    carry = lax.fori_loop(0, steps, step, start, unroll=unroll)
    if flush:
        row = row_start + 8 * (steps - 1)
        for w in cols:
            _, old_flux, old_gain = carry[w]
            for f, g, o in zip((0, lane_flow, row_flow), old_gain, old_flux):
                dst[f, w, row : row + 8, :] = src[f, w, row : row + 8, :] + TIME_STEP * (g - o)


def load_kernel(depth, velocity, bed, state, water, speed, ground, sems):
    copies = [
        pltpu.make_async_copy(depth, water, sems.at[0]),
        pltpu.make_async_copy(velocity, speed, sems.at[1]),
        pltpu.make_async_copy(bed, ground, sems.at[2]),
    ]
    for copy in copies:
        copy.start()
    for copy in copies:
        copy.wait()
    for w in range(CT):
        cols = slice(w * TILE, (w + 1) * TILE)
        for r in range(0, ROWS, 8):
            rows = slice(r, r + 8)
            here = water[rows, cols]
            state[0, w, rows, :] = here
            state[1, w, rows, :] = here * speed[0, rows, cols]
            state[2, w, rows, :] = here * speed[1, rows, cols]
            state[3, w, rows, :] = ground[rows, cols]


class Lists:
    def __init__(self, listed, partner):
        self.rows = lax.axis_index("rows")
        self.cols = lax.axis_index("cols")
        self.span = CT * lax.axis_size("cols")
        self.ids = [
            (self.rows * RT + t // CT) * self.span + self.cols * CT + t % CT for t in range(RT * CT)
        ]
        self.listed = [listed[k] for k in range(SLOTS)]
        self.partner = [partner[k] for k in range(SLOTS)]

    def inside(self, entry):
        found = [entry == i for i in self.ids]
        any_found = found[0]
        local = jnp.int32(0)
        for t in range(1, RT * CT):
            any_found = any_found | found[t]
            local = jnp.where(found[t], jnp.int32(t), local)
        return any_found, local

    def active(self, t):
        hit = self.listed[0] == self.ids[t]
        for entry in self.listed[1:] + self.partner:
            hit = hit | (entry == self.ids[t])
        return hit

    def outgoing(self):
        used = [jnp.bool_(False)] * MOVED
        tile = [jnp.int32(0)] * MOVED
        rank = jnp.int32(0)
        for entry in self.partner:
            own, local = self.inside(entry)
            for k in range(MOVED):
                take = own & (rank == k)
                used[k] = used[k] | take
                tile[k] = jnp.where(take, local, tile[k])
            rank = rank + own.astype(jnp.int32)
        return used, tile

    def kept(self):
        used = [jnp.bool_(False)] * MOVED
        tile = [jnp.int32(0)] * MOVED
        rank = jnp.int32(0)
        for entry in self.listed:
            own, local = self.inside(entry)
            for k in range(MOVED):
                take = own & (rank == k)
                used[k] = used[k] | take
                tile[k] = jnp.where(take, local, tile[k])
            rank = rank + own.astype(jnp.int32)
        return used, tile


def edge_kernel(listed, partner, state, strips, inner):
    lists = Lists(listed, partner)
    lane = lax.broadcasted_iota(jnp.int32, (TILE, TILE), 1)
    for f in range(4):
        for w in range(CT):
            cols = slice(w * TILE, (w + 1) * TILE)
            strips[f, 0:8, cols] = state[f, w, ROWS - 8 : ROWS, :]
            strips[f, 8:16, cols] = state[f, w, 0:8, :]
        for r in range(RT):
            rows = slice(r * TILE, (r + 1) * TILE)
            cols = slice(r * TILE, (r + 1) * TILE)
            one, two = state[f, 0, rows, :], state[f, CT - 1, rows, :]
            turned = jnp.where(lane < TILE // 2, one, two).T
            strips[f, 16:24, cols] = turned[TILE - 8 :, :]
            strips[f, 24:32, cols] = turned[:8, :]
            turned = jnp.where(lane < TILE // 2, two, one).T
            inner[f, 0:8, cols] = turned[TILE - 8 :, :]
            inner[f, 8:16, cols] = turned[:8, :]
    flags = [jnp.where(lists.active(t), 1.0, 0.0) for t in range(RT * CT)]

    def full(t):
        return jnp.full((8, TILE), flags[t], jnp.float32)

    for w in range(CT):
        cols = slice(w * TILE, (w + 1) * TILE)
        strips[4, 0:8, cols] = full((RT - 1) * CT + w)
        strips[4, 8:16, cols] = full(w)
    for r in range(RT):
        cols = slice(r * TILE, (r + 1) * TILE)
        strips[4, 16:24, cols] = full(r * CT + CT - 1)
        strips[4, 24:32, cols] = full(r * CT)
        inner[4, 0:8, cols] = full(r * CT)
        inner[4, 8:16, cols] = full(r * CT + CT - 1)


def wide_kernel(mine, other, out):
    is_left = lax.axis_index("cols") == 0
    for f in range(5):
        own = jnp.where(is_left, mine[f, 8:12, :], mine[f, 4:8, :])
        near = jnp.where(is_left, other[f, 8:12, :], other[f, 4:8, :])
        out[4 * f : 4 * f + 4, 0:COLS] = jnp.where(is_left, own, near)
        out[4 * f : 4 * f + 4, COLS : 2 * COLS] = jnp.where(is_left, near, own)
    out[20:24, :] = jnp.zeros((4, 2 * COLS), jnp.float32)


def halo_rows(came, near, f, upper, is_left):
    rows = slice(4 * f, 4 * f + 4)
    return jnp.where(is_left == upper, came[rows, :], near[rows, :])


def gather_pair(tile, state, mine, came, near, start):
    is_left = lax.axis_index("cols") == 0
    blank = jnp.zeros((4, TILE), jnp.float32)
    for k in range(MOVED):
        r, c = tile[k] // CT, tile[k] % CT
        base = pl.multiple_of(r * TILE, TILE)
        for f in range(4):
            start[f, k, PAD : PAD + TILE, :] = state[f, c, pl.ds(base, TILE), :]
        for f in range(5):
            above = halo_rows(came, near, f, True, is_left)
            below = halo_rows(came, near, f, False, is_left)
            ends = []
            for halo in (above, below):
                pieces = [halo[:, q * TILE : (q + 1) * TILE] for q in range(2 * CT)]
                first = jnp.where(is_left, pieces[0], pieces[2])
                second = jnp.where(is_left, pieces[1], pieces[3])
                ends.append(jnp.where(c == 0, first, second))

            @pl.when(r == 0)
            def _(f=f, k=k, c=c, ends=ends):
                start[f, k, PAD - 8 : PAD - 4, :] = blank
                start[f, k, PAD - 4 : PAD, :] = ends[0]
                if f < 4:
                    start[f, k, PAD + TILE : PAD + TILE + 8, :] = state[f, c, TILE : TILE + 8, :]
                else:
                    flag = jnp.where(c == 0, mine[4, 0:8, 0:TILE], mine[4, 0:8, TILE : 2 * TILE])
                    start[f, k, PAD + TILE : PAD + TILE + 8, :] = flag

            @pl.when(r == RT - 1)
            def _(f=f, k=k, c=c, ends=ends):
                start[f, k, PAD + TILE : PAD + TILE + 4, :] = ends[1]
                start[f, k, PAD + TILE + 4 : PAD + TILE + 8, :] = blank
                if f < 4:
                    start[f, k, PAD - 8 : PAD, :] = state[f, c, TILE - 8 : TILE, :]
                else:
                    flag = jnp.where(c == 0, mine[4, 8:16, 0:TILE], mine[4, 8:16, TILE : 2 * TILE])
                    start[f, k, PAD - 8 : PAD, :] = flag


def still(dst, src, width, rows):
    for w in range(width):
        alive = src[4, w, rows, :] > 0.5
        for f in range(3):
            dst[f, w, rows, :] = jnp.where(alive, dst[f, w, rows, :], src[f, w, rows, :])


def advance_pair(start, middle, end, first, last, unroll):
    steps = (last - first) // 8 + 2
    row = PAD + first - 8
    sweep(start, start, middle, MOVED, steps, row, 1, 2, unroll, True)
    if first == 0:
        still(middle, start, MOVED, slice(PAD - 8, PAD))
    if last == TILE:
        still(middle, start, MOVED, slice(PAD + TILE, PAD + TILE + 8))
    sweep(middle, start, end, MOVED, steps, row, 1, 2, unroll, False)


def overlay(cell, fix, board, store):
    lane = lax.broadcasted_iota(jnp.int32, (8, TILE), 1)
    for f in range(3):
        board[8 * f : 8 * f + 8, :] = fix(f)
    turned = board[...].T
    for f in range(3):
        for b in range(0, TILE, 8):
            strip = turned[b : b + 8, :]
            left = pltpu.roll(strip, (TILE - 8 * f) % TILE, 1)
            right = pltpu.roll(strip, TILE - 8 - 8 * f, 1)
            value = jnp.where(lane < REACH, left, cell(f, b))
            store(f, b, jnp.where(lane >= TILE - REACH, right, value))


def upper_kernel(listed, partner, state, mine, came, near, start, out, middle, end):
    _, tile = Lists(listed, partner).outgoing()
    gather_pair(tile, state, mine, came, near, start)
    advance_pair(start, middle, end, 0, PART, UNROLL_PART)
    for k in range(MOVED):
        for f in range(3):
            out[k, f] = end[f, k, PAD : PAD + PART, :]


def lower_kernel(listed, partner, start, fixes, out, middle, end):
    _, tile = Lists(listed, partner).outgoing()
    advance_pair(start, middle, end, PART, TILE, UNROLL_PART)
    for k in range(MOVED):
        for f in range(3):
            out[k, f, 0:PART, :] = end[f, k, PAD + PART : PAD + TILE, :]
            out[k, f, PART : PART + 8, :] = fixes[tile[k], f]


def keep_kernel(listed, partner, state, mine, came, near, fixes, after, out, start, middle, end, board):
    del after
    used, tile = Lists(listed, partner).kept()

    @pl.when(used[0])
    def _():
        gather_pair(tile, state, mine, came, near, start)
        advance_pair(start, middle, end, 0, TILE, UNROLL_FULL)
        board[...] = jnp.zeros_like(board)
        for k in range(MOVED):

            def store(f, b, value, k=k):
                out[k, f, b : b + 8, :] = value

            overlay(
                lambda f, b, k=k: end[f, k, PAD + b : PAD + b + 8, :],
                lambda f, k=k: fixes[tile[k], f],
                board,
                store,
            )


def seam_kernel(mine, other, inner, came, near, after, fixes, start, middle, end, one, two, side, board):
    del after
    is_left = lax.axis_index("cols") == 0
    lane = lax.broadcasted_iota(jnp.int32, (8, TILE), 1)
    for f in range(5):
        for w in range(CT):
            cols = slice(w * TILE, (w + 1) * TILE)
            start[f, w, PAD : PAD + 8, :] = mine[f, 16:24, cols]
            start[f, w, PAD + 8 : PAD + 12, :] = jnp.where(is_left, other[f, 24:28, cols], 0.0)
            start[f, w, PAD + 12 : PAD + 16, :] = jnp.where(is_left, 0.0, other[f, 20:24, cols])
            start[f, w, PAD + 16 : PAD + 24, :] = mine[f, 24:32, cols]
            start[f, w, PAD + 24 : PAD + 40, :] = inner[f, :, cols]
        for place, upper in ((0, False), (4, True)):
            halo = halo_rows(came, near, f, upper, is_left)
            pieces = [halo[:, q * TILE : (q + 1) * TILE] for q in range(2 * CT)]
            rows = slice(8 * f + place, 8 * f + place + 4)
            one[rows, :] = jnp.where(is_left, pieces[0], pieces[2])
            two[rows, :] = jnp.where(is_left, pieces[1], pieces[3])
            side[rows, :] = jnp.where(is_left, pieces[2], pieces[1])
    board[...] = jnp.zeros_like(board)
    for b in range(0, 40, 8):
        rows = slice(b, b + 8)
        first, second, beside = one[rows, :], two[rows, :], side[rows, :]
        value = jnp.where(lane < 8, pltpu.roll(second, 8, 1), 0.0)
        value = jnp.where((lane >= 8) & (lane < 12) & is_left, pltpu.roll(beside, 8, 1), value)
        far = jnp.logical_not(is_left)
        value = jnp.where((lane >= 12) & (lane < 16) & far, pltpu.roll(beside, 16, 1), value)
        value = jnp.where((lane >= 16) & (lane < 24), pltpu.roll(first, 16, 1), value)
        value = jnp.where((lane >= 24) & (lane < 32), pltpu.roll(first, 32, 1), value)
        board[rows, :] = jnp.where((lane >= 32) & (lane < 40), pltpu.roll(second, 32, 1), value)
    turned = board[...].T
    for f in range(5):
        for b in range(0, SEAM, 8):
            rows = slice(PAD + b, PAD + b + 8)
            first, second = start[f, 0, rows, :], start[f, 1, rows, :]
            ends = pltpu.roll(turned[b : b + 8, :], (8 - 8 * f) % TILE, 1)
            value = jnp.where(lane < 8, pltpu.roll(second, 8, 1), 0.0)
            value = jnp.where((lane >= 8) & (lane < 16), ends, value)
            value = jnp.where((lane >= 16) & (lane < 24), pltpu.roll(first, 16, 1), value)
            value = jnp.where((lane >= 24) & (lane < 32), pltpu.roll(first, 32, 1), value)
            start[f, CT, rows, :] = jnp.where(
                (lane >= 32) & (lane < 40), pltpu.roll(second, 32, 1), value
            )
    width = CT + 1
    sweep(start, start, middle, width, SEAM // 8, PAD, 2, 1, UNROLL_SEAM, True)
    still(middle, start, width, slice(PAD, PAD + SEAM))
    sweep(middle, start, end, width, SEAM // 8, PAD, 2, 1, UNROLL_SEAM, True)
    lane = lax.broadcasted_iota(jnp.int32, (4, TILE), 1)
    for t in range(RT * CT):
        r, c = t // CT, t % CT
        for place, row in ((0, 16 if c == 0 else 32), (4, 28 if c == 0 else 4)):
            rows = slice(PAD + row, PAD + row + 4)
            for f in range(3):
                ends = end[f, CT, rows, :]
                low = pltpu.roll(ends, 112 if r == 0 else 96, 1)
                high = pltpu.roll(ends, 96 if r == 0 else 120, 1)
                value = jnp.where(lane < REACH, low, end[f, r, rows, :])
                fixes[t, f, place : place + 4, :] = jnp.where(lane >= TILE - REACH, high, value)


def pack_kernel(listed, partner, kept, upper, lower, packed, board):
    lists = Lists(listed, partner)
    board[...] = jnp.zeros_like(board)
    far = jnp.int32(0)
    near = jnp.int32(0)
    for s in range(SLOTS):
        entry = lists.listed[s]
        own, _ = lists.inside(entry)
        foreign = (entry >= 0) & jnp.logical_not(own)
        here = jnp.minimum(near, MOVED - 1)
        there = jnp.minimum(far, MOVED - 1)
        near = near + own.astype(jnp.int32)
        far = far + foreign.astype(jnp.int32)

        @pl.when(own)
        def _(s=s, here=here):
            packed[s] = kept[here]

        @pl.when(foreign)
        def _(s=s, there=there):
            def cell(f, b):
                if b < PART:
                    return upper[there, f, b : b + 8, :]
                return lower[there, f, b - PART : b - PART + 8, :]

            def store(f, b, value):
                packed[s, f, b : b + 8, :] = value

            overlay(cell, lambda f: lower[there, f, PART : PART + 8, :], board, store)

        @pl.when(entry < 0)
        def _(s=s):
            packed[s] = jnp.zeros((3, TILE, TILE), jnp.float32)


def passed_along(block, distance):
    count = lax.axis_size("rows")
    return lax.ppermute(block, "rows", [((i - distance) % count, i) for i in range(count)])


def swapped(block):
    return lax.ppermute(block, "cols", [(0, 1), (1, 0)])


def scratch(*shape):
    return pltpu.VMEM(shape, jnp.float32)


def shards(depth, velocity, bed, slots):
    count = lax.axis_size("rows")
    half = count // 2
    listed = slots[0, 0]
    partner = passed_along(listed, half)
    (state,) = call(
        load_kernel,
        [HBM] * 3,
        [f32(4, CT, ROWS, TILE)],
        [
            scratch(ROWS, COLS),
            scratch(2, ROWS, COLS),
            scratch(ROWS, COLS),
            pltpu.SemaphoreType.DMA((3,)),
        ],
    )(depth, velocity, bed)
    mine, inner = call(
        edge_kernel, [SMEM, SMEM, VMEM], [f32(5, 32, COLS), f32(5, 16, COLS)]
    )(listed, partner, state)
    other = swapped(mine)
    (wide,) = call(wide_kernel, [VMEM, VMEM], [f32(24, 2 * COLS)])(mine, other)
    route = [(2 * r, 2 * r - 1) for r in range(1, count)]
    route += [(2 * r + 1, 2 * r + 2) for r in range(count - 1)]
    came = lax.ppermute(wide, ("rows", "cols"), route)
    near = swapped(came)
    pair = [scratch(3, MOVED, SPAN, TILE)] * 2
    start, upper = call(
        upper_kernel,
        [SMEM, SMEM] + [VMEM] * 4,
        [f32(5, MOVED, SPAN, TILE), f32(MOVED, 3, PART, TILE)],
        pair,
    )(listed, partner, state, mine, came, near)
    far_upper = passed_along(upper, half)
    (fixes,) = call(
        seam_kernel,
        [VMEM] * 5 + [pl.BlockSpec(memory_space=pl.ANY)],
        [f32(RT * CT, 3, 8, TILE)],
        [scratch(5, CT + 1, SEAM_DEEP, TILE)]
        + [scratch(3, CT + 1, SEAM_DEEP, TILE)] * 2
        + [scratch(40, TILE)] * 3
        + [scratch(TILE, TILE)],
    )(mine, other, inner, came, near, upper)
    (lower,) = call(
        lower_kernel, [SMEM, SMEM, VMEM, VMEM], [f32(MOVED, 3, PART + 8, TILE)], pair
    )(listed, partner, start, fixes)
    far_lower = passed_along(lower, half)
    (kept,) = call(
        keep_kernel,
        [SMEM, SMEM] + [VMEM] * 5 + [pl.BlockSpec(memory_space=pl.ANY)],
        [f32(MOVED, 3, TILE, TILE)],
        [scratch(5, MOVED, SPAN, TILE)] + pair + [scratch(TILE, TILE)],
    )(listed, partner, state, mine, came, near, fixes, lower)
    (packed,) = call(
        pack_kernel, [SMEM, SMEM] + [VMEM] * 3, [f32(SLOTS, 3, TILE, TILE)], [scratch(TILE, TILE)]
    )(listed, partner, kept, far_upper, far_lower)
    return packed[None, None]


def solution(mesh):
    in_specs = (
        P(("groups", "rows"), "cols"),
        P(None, ("groups", "rows"), "cols"),
        P(("groups", "rows"), "cols"),
        P(("groups", "rows"), "cols", None),
    )
    out_specs = P(("groups", "rows"), "cols", None, None, None, None)

    return jax.shard_map(shards, mesh=mesh, in_specs=in_specs, out_specs=out_specs, check_vma=False)
```

```python
import jax
import jax.numpy as jnp
from jax import lax
from jax.experimental import pallas as pl
from jax.experimental.pallas import tpu as pltpu
from jax.sharding import PartitionSpec as P


TILE = 128
RT = 2
CT = 2
SLOTS = 3
MOVED = RT * CT // 2
ROWS = RT * TILE
COLS = CT * TILE
PAD = 16
SEAM = 40
SEAM_DEEP = SEAM + 2 * PAD
SPAN = TILE + 2 * PAD
INNER = 80
OUTER = TILE - INNER
REACH = 4
UNROLL_INNER = 3
UNROLL_OUTER = 2
UNROLL_FULL = 3
UNROLL_SEAM = 1

GRAVITY = 9.81
TIME_STEP = 0.04
DRY_DEPTH = 0.05
SPEED_FLOOR = 0.5
ROOT_GRAVITY = GRAVITY**0.5
TINY = 1.2e-38

VMEM = pl.BlockSpec(memory_space=pltpu.VMEM)
HBM = pl.BlockSpec(memory_space=pltpu.HBM)
SMEM = pl.BlockSpec(memory_space=pltpu.SMEM)


def f32(*shape):
    return jax.ShapeDtypeStruct(shape, jnp.float32)


def call(kernel, ins, outs, scratch=(), room=20 * 2**20):
    return pl.pallas_call(
        kernel,
        in_specs=list(ins),
        out_specs=tuple(VMEM for _ in outs),
        out_shape=tuple(outs),
        scratch_shapes=list(scratch),
        compiler_params=pltpu.CompilerParams(vmem_limit_bytes=room),
    )


def limited(down, up):
    return 0.5 * jnp.maximum(jnp.minimum(down, jnp.maximum(up, 0.0)), jnp.minimum(up, 0.0))


def speeds(water, normal, across):
    square = water * water
    factor = (water + water) / (square + jnp.maximum(square, DRY_DEPTH * DRY_DEPTH))
    return factor * normal, factor * across


def wave_speed(level):
    return (ROOT_GRAVITY * level) * lax.rsqrt(jnp.maximum(level, TINY))


def face_flux(left, right):
    water_l, speed_l, drift_l, ground_l = left
    water_r, speed_r, drift_r, ground_r = right
    top = jnp.maximum(ground_l, ground_r)
    level_l = jnp.maximum(water_l + (ground_l - top), 0.0)
    level_r = jnp.maximum(water_r + (ground_r - top), 0.0)
    wave_l = wave_speed(level_l)
    wave_r = wave_speed(level_r)
    lower = jnp.minimum(jnp.minimum(speed_l - wave_l, speed_r - wave_r), 0.0)
    upper = jnp.maximum(jnp.maximum(speed_l + wave_l, speed_r + wave_r), 0.0)
    inverse = 1.0 / jnp.maximum(upper - lower, SPEED_FLOOR)
    up = upper * inverse
    low = lower * inverse
    both = upper * low
    part_l = level_l * (up * speed_l - both)
    part_r = level_r * (both - low * speed_r)
    press_l = (0.5 * GRAVITY) * (level_l * level_l)
    press_r = (0.5 * GRAVITY) * (level_r * level_r)
    mass = part_l + part_r
    push = part_l * speed_l + part_r * speed_r + up * press_l - low * press_r
    side = part_l * drift_l + part_r * drift_r
    return mass, push - press_l, push - press_r, side


def sweep(src, ground, dst, width, steps, starts, lane_flow, row_flow, unroll, flush):
    sub = lax.broadcasted_iota(jnp.int32, (8, 128), 0)
    cols = range(width)

    def step(i, carry):
        shift = pl.multiple_of(i * 8, 8)

        def read(f, w, offset):
            held = src if f < 3 else ground
            return held[f, w, pl.ds(shift + starts[w] + offset, 8), :]

        now = []
        for w in cols:
            x = [read(f, w, 0) for f in range(4)]
            low, high, half = [], [], []
            for f in (0, lane_flow, row_flow, 3):
                down = x[f] - pltpu.roll(x[f], 1, 1)
                hs = limited(down, pltpu.roll(down, TILE - 1, 1))
                low.append(x[f] - hs)
                high.append(x[f] + hs)
                half.append(hs)
            fast = speeds(high[0], high[1], high[2])
            slow = speeds(low[0], low[1], low[2])
            left = [pltpu.roll(v, 1, 1) for v in (high[0], fast[0], fast[1], high[3])]
            mass, push_l, push_r, side = face_flux(left, (low[0], slow[0], slow[1], low[3]))
            weight = (2.0 * GRAVITY) * x[0]
            gain_water = mass - pltpu.roll(mass, TILE - 1, 1)
            gain_lane = push_r - pltpu.roll(push_l, TILE - 1, 1) - weight * (half[0] + half[3])
            gain_row = side - pltpu.roll(side, TILE - 1, 1)
            low, high, half = [], [], []
            for f in (0, row_flow, lane_flow, 3):
                hs = limited(x[f] - read(f, w, -1), read(f, w, 1) - x[f])
                low.append(x[f] - hs)
                high.append(x[f] + hs)
                half.append(hs)
            fast = speeds(high[0], high[1], high[2])
            slow = speeds(low[0], low[1], low[2])
            old_high, old_flux, old_gain = carry[w]
            high_now = tuple(pltpu.roll(v, 1, 0) for v in (high[0], fast[0], fast[1], high[3]))
            left = [jnp.where(sub == 0, o, n) for o, n in zip(old_high, high_now)]
            mass, push_l, push_r, side = face_flux(left, (low[0], slow[0], slow[1], low[3]))
            gain = (
                gain_water + mass,
                gain_lane + side,
                gain_row + push_r - weight * (half[0] + half[3]),
            )
            flux_now = tuple(pltpu.roll(v, 7, 0) for v in (mass, side, push_l))
            for f, g, o, n in zip((0, lane_flow, row_flow), old_gain, old_flux, flux_now):
                dst[f, w, pl.ds(shift + starts[w] - 8, 8), :] = read(f, w, -8) + TIME_STEP * (
                    g - jnp.where(sub == 7, n, o)
                )
            now.append((high_now, flux_now, gain))
        return tuple(now)

    zero = jnp.zeros((8, 128), jnp.float32)
    start = tuple(((zero,) * 4, (zero,) * 3, (zero,) * 3) for _ in cols)
    carry = lax.fori_loop(0, steps, step, start, unroll=unroll)
    if flush:
        for w in cols:
            rows = pl.ds(starts[w] + 8 * (steps - 1), 8)
            _, old_flux, old_gain = carry[w]
            for f, g, o in zip((0, lane_flow, row_flow), old_gain, old_flux):
                dst[f, w, rows, :] = src[f, w, rows, :] + TIME_STEP * (g - o)


def load_kernel(depth, velocity, bed, state, turned, water, speed, ground, sems):
    copies = [
        pltpu.make_async_copy(depth, water, sems.at[0]),
        pltpu.make_async_copy(velocity, speed, sems.at[1]),
        pltpu.make_async_copy(bed, ground, sems.at[2]),
    ]
    for copy in copies:
        copy.start()
    for copy in copies:
        copy.wait()
    for w in range(CT):
        cols = slice(w * TILE, (w + 1) * TILE)
        for r in range(0, ROWS, 8):
            rows = slice(r, r + 8)
            here = water[rows, cols]
            state[0, w, rows, :] = here
            state[1, w, rows, :] = here * speed[0, rows, cols]
            state[2, w, rows, :] = here * speed[1, rows, cols]
            state[3, w, rows, :] = ground[rows, cols]
    lane = lax.broadcasted_iota(jnp.int32, (TILE, TILE), 1)
    for f in range(4):
        for r in range(RT):
            held = slice(r * TILE, (r + 1) * TILE)
            one, two = state[f, 0, held, :], state[f, CT - 1, held, :]
            flipped = jnp.where(lane < TILE // 2, one, two).T
            turned[f, 0:8, held] = flipped[TILE - 8 :, :]
            turned[f, 8:16, held] = flipped[:8, :]
            flipped = jnp.where(lane < TILE // 2, two, one).T
            turned[f, 16:24, held] = flipped[TILE - 8 :, :]
            turned[f, 24:32, held] = flipped[:8, :]


class Lists:
    def __init__(self, lists):
        self.rows = lax.axis_index("rows")
        self.cols = lax.axis_index("cols")
        self.span = CT * lax.axis_size("cols")
        self.ids = [
            (self.rows * RT + t // CT) * self.span + self.cols * CT + t % CT for t in range(RT * CT)
        ]
        self.listed = [lists[k] for k in range(SLOTS)]
        self.partner = [lists[SLOTS + k] for k in range(SLOTS)]

    def inside(self, entry):
        found = [entry == i for i in self.ids]
        any_found = found[0]
        local = jnp.int32(0)
        for t in range(1, RT * CT):
            any_found = any_found | found[t]
            local = jnp.where(found[t], jnp.int32(t), local)
        return any_found, local

    def active(self, t):
        hit = self.listed[0] == self.ids[t]
        for entry in self.listed[1:] + self.partner:
            hit = hit | (entry == self.ids[t])
        return hit

    def flags(self):
        return [jnp.where(self.active(t), 1.0, 0.0) for t in range(RT * CT)]

    def outgoing(self):
        used = [jnp.bool_(False)] * MOVED
        tile = [jnp.int32(0)] * MOVED
        rank = jnp.int32(0)
        for entry in self.partner:
            own, local = self.inside(entry)
            for k in range(MOVED):
                take = own & (rank == k)
                used[k] = used[k] | take
                tile[k] = jnp.where(take, local, tile[k])
            rank = rank + own.astype(jnp.int32)
        return used, tile

    def kept(self):
        used = [jnp.bool_(False)] * MOVED
        tile = [jnp.int32(0)] * MOVED
        rank = jnp.int32(0)
        for entry in self.listed:
            own, local = self.inside(entry)
            for k in range(MOVED):
                take = own & (rank == k)
                used[k] = used[k] | take
                tile[k] = jnp.where(take, local, tile[k])
            rank = rank + own.astype(jnp.int32)
        return used, tile


def edge_kernel(lists, state, turned, own, out):
    lists = Lists(lists)
    is_left = lists.cols == 0
    flags = lists.flags()
    for w in range(CT):
        cols = slice(w * TILE, (w + 1) * TILE)
        for f in range(4):
            rows = slice(4 * f, 4 * f + 4)
            first = state[f, w, 0:REACH, :]
            last = state[f, w, ROWS - REACH : ROWS, :]
            own[rows, cols] = jnp.where(is_left, first, last)
            out[rows, cols] = jnp.where(is_left, last, first)
        first, last = flags[w], flags[(RT - 1) * CT + w]
        own[16:24, cols] = jnp.full((8, TILE), jnp.where(is_left, first, last), jnp.float32)
        out[16:24, cols] = jnp.full((8, TILE), jnp.where(is_left, last, first), jnp.float32)
    for f in range(4):
        rows = slice(24 + 4 * f, 28 + 4 * f)
        out[rows, :] = jnp.where(is_left, turned[f, 4:8, :], turned[f, 8:12, :])
    for r in range(RT):
        flag = jnp.where(is_left, flags[r * CT + CT - 1], flags[r * CT])
        out[40:48, r * TILE : (r + 1) * TILE] = jnp.full((8, TILE), flag, jnp.float32)


def wide_kernel(own, other, out):
    is_left = lax.axis_index("cols") == 0
    near = other[0:24, :]
    out[:, 0:COLS] = jnp.where(is_left, own[...], near)
    out[:, COLS : 2 * COLS] = jnp.where(is_left, near, own[...])


def halo_pieces(came, near, f, upper):
    is_left = lax.axis_index("cols") == 0
    rows = slice(4 * f, 4 * f + 4)
    halo = jnp.where(is_left == upper, came[rows, :], near[rows, :])
    part = [halo[:, q * TILE : (q + 1) * TILE] for q in range(2 * CT)]
    return (
        jnp.where(is_left, part[0], part[2]),
        jnp.where(is_left, part[1], part[3]),
        jnp.where(is_left, part[2], part[1]),
    )


def gather_pair(tile, flags, state, start, halos):
    blank = jnp.zeros((4, TILE), jnp.float32)
    over = slice(PAD - 8, PAD)
    under = slice(PAD + TILE, PAD + TILE + 8)
    for k in range(MOVED):
        r, c = tile[k] // CT, tile[k] % CT
        base = pl.multiple_of(r * TILE, TILE)
        for f in range(4):
            start[f, k, PAD : PAD + TILE, :] = state[f, c, pl.ds(base, TILE), :]
        if halos is not None:
            ends = [
                [jnp.where(c == 0, *halo_pieces(*halos, f, upper)[:2]) for f in range(5)]
                for upper in (True, False)
            ]

        @pl.when(r == 0)
        def _(k=k, c=c):
            for f in range(4):
                start[f, k, under, :] = state[f, c, TILE : TILE + 8, :]
            flag = jnp.where(c == 0, flags[CT], flags[CT + 1])
            start[4, k, under, :] = jnp.full((8, TILE), flag, jnp.float32)
            if halos is not None:
                for f in range(5):
                    start[f, k, PAD - 8 : PAD - 4, :] = blank
                    start[f, k, PAD - 4 : PAD, :] = ends[0][f]

        @pl.when(r == RT - 1)
        def _(k=k, c=c):
            for f in range(4):
                start[f, k, over, :] = state[f, c, TILE - 8 : TILE, :]
            flag = jnp.where(c == 0, flags[0], flags[1])
            start[4, k, over, :] = jnp.full((8, TILE), flag, jnp.float32)
            if halos is not None:
                for f in range(5):
                    start[f, k, PAD + TILE : PAD + TILE + 4, :] = ends[1][f]
                    start[f, k, PAD + TILE + 4 : PAD + TILE + 8, :] = blank


def still(dst, src, width, rows):
    for w in range(width):
        alive = src[4, w, rows, :] > 0.5
        for f in range(3):
            dst[f, w, rows, :] = jnp.where(alive, dst[f, w, rows, :], src[f, w, rows, :])


def aligned(row):
    return row if isinstance(row, int) else pl.multiple_of(row, 8)


def advance_pair(start, middle, end, firsts, count, masked, unroll):
    steps = count // 8 + 2
    starts = [aligned(first) + (PAD - 8) for first in firsts]
    sweep(start, start, middle, MOVED, steps, starts, 1, 2, unroll, True)
    for w in range(MOVED):
        for row in masked[w]:
            rows = pl.ds(aligned(row) + PAD, 8)
            alive = start[4, w, rows, :] > 0.5
            for f in range(3):
                middle[f, w, rows, :] = jnp.where(alive, middle[f, w, rows, :], start[f, w, rows, :])
    sweep(middle, start, end, MOVED, steps, starts, 1, 2, unroll, False)


def overlay(cell, fix, board, store):
    lane = lax.broadcasted_iota(jnp.int32, (8, TILE), 1)
    for f in range(3):
        board[8 * f : 8 * f + 8, :] = fix(f)
    turned = board[...].T
    for f in range(3):
        for b in range(0, TILE, 8):
            strip = turned[b : b + 8, :]
            left = pltpu.roll(strip, (TILE - 8 * f) % TILE, 1)
            right = pltpu.roll(strip, TILE - 8 - 8 * f, 1)
            value = jnp.where(lane < REACH, left, cell(f, b))
            store(f, b, jnp.where(lane >= TILE - REACH, right, value))


def inner_kernel(lists, state, out, start, middle, end):
    lists = Lists(lists)
    _, tile = lists.outgoing()
    gather_pair(tile, lists.flags(), state, start, None)
    top = [t // CT == 0 for t in tile]
    firsts = [jnp.where(u, OUTER, 0) for u in top]
    masked = [[jnp.where(u, TILE, -8)] for u in top]
    advance_pair(start, middle, end, firsts, INNER, masked, UNROLL_INNER)
    for k in range(MOVED):
        rows = pl.ds(pl.multiple_of(firsts[k], 8) + PAD, INNER)
        for f in range(3):
            out[k, f] = end[f, k, rows, :]


def outer_kernel(lists, state, came, near, fixes, out, start, middle, end):
    lists = Lists(lists)
    _, tile = lists.outgoing()
    gather_pair(tile, lists.flags(), state, start, (came, near))
    top = [t // CT == 0 for t in tile]
    firsts = [jnp.where(u, 0, INNER) for u in top]
    masked = [[jnp.where(u, -8, TILE)] for u in top]
    advance_pair(start, middle, end, firsts, OUTER, masked, UNROLL_OUTER)
    for k in range(MOVED):
        rows = pl.ds(pl.multiple_of(firsts[k], 8) + PAD, OUTER)
        for f in range(3):
            out[k, f, 0:OUTER, :] = end[f, k, rows, :]
            out[k, f, OUTER : OUTER + 8, :] = fixes[tile[k], f]


def keep_kernel(lists, state, came, near, fixes, out, start, middle, end, board):
    lists = Lists(lists)
    used, tile = lists.kept()

    @pl.when(used[0])
    def _():
        gather_pair(tile, lists.flags(), state, start, (came, near))
        masked = [[-8, TILE]] * MOVED
        advance_pair(start, middle, end, [0] * MOVED, TILE, masked, UNROLL_FULL)
        board[...] = jnp.zeros_like(board)
        for k in range(MOVED):

            def store(f, b, value, k=k):
                out[k, f, b : b + 8, :] = value

            overlay(
                lambda f, b, k=k: end[f, k, PAD + b : PAD + b + 8, :],
                lambda f, k=k: fixes[tile[k], f],
                board,
                store,
            )


def seam_kernel(lists, turned, other, came, near, fixes, start, middle, end, one, two, side, board):
    lists = Lists(lists)
    is_left = lists.cols == 0
    flags = lists.flags()
    lane = lax.broadcasted_iota(jnp.int32, (8, TILE), 1)
    for w in range(CT):
        cols = slice(w * TILE, (w + 1) * TILE)
        for f in range(5):
            beside = other[24 + 4 * f : 28 + 4 * f, cols]
            start[f, w, PAD + 8 : PAD + 12, :] = jnp.where(is_left, beside, 0.0)
            start[f, w, PAD + 12 : PAD + 16, :] = jnp.where(is_left, 0.0, beside)
            if f < 4:
                start[f, w, PAD : PAD + 8, :] = turned[f, 0:8, cols]
                start[f, w, PAD + 16 : PAD + 40, :] = turned[f, 8:32, cols]
        for row, c in ((0, CT - 1), (16, 0), (24, 0), (32, CT - 1)):
            full = jnp.full((8, TILE), flags[w * CT + c], jnp.float32)
            start[4, w, PAD + row : PAD + row + 8, :] = full
    for f in range(5):
        for place, upper in ((0, False), (4, True)):
            rows = slice(8 * f + place, 8 * f + place + 4)
            pieces = halo_pieces(came, near, f, upper)
            one[rows, :], two[rows, :], side[rows, :] = pieces
    board[...] = jnp.zeros_like(board)
    for b in range(0, 40, 8):
        rows = slice(b, b + 8)
        first, second, beside = one[rows, :], two[rows, :], side[rows, :]
        value = jnp.where(lane < 8, pltpu.roll(second, 8, 1), 0.0)
        value = jnp.where((lane >= 8) & (lane < 12) & is_left, pltpu.roll(beside, 8, 1), value)
        far = jnp.logical_not(is_left)
        value = jnp.where((lane >= 12) & (lane < 16) & far, pltpu.roll(beside, 16, 1), value)
        value = jnp.where((lane >= 16) & (lane < 24), pltpu.roll(first, 16, 1), value)
        value = jnp.where((lane >= 24) & (lane < 32), pltpu.roll(first, 32, 1), value)
        board[rows, :] = jnp.where((lane >= 32) & (lane < 40), pltpu.roll(second, 32, 1), value)
    turned = board[...].T
    for f in range(5):
        for b in range(0, SEAM, 8):
            rows = slice(PAD + b, PAD + b + 8)
            first, second = start[f, 0, rows, :], start[f, 1, rows, :]
            ends = pltpu.roll(turned[b : b + 8, :], (8 - 8 * f) % TILE, 1)
            value = jnp.where(lane < 8, pltpu.roll(second, 8, 1), 0.0)
            value = jnp.where((lane >= 8) & (lane < 16), ends, value)
            value = jnp.where((lane >= 16) & (lane < 24), pltpu.roll(first, 16, 1), value)
            value = jnp.where((lane >= 24) & (lane < 32), pltpu.roll(first, 32, 1), value)
            start[f, CT, rows, :] = jnp.where(
                (lane >= 32) & (lane < 40), pltpu.roll(second, 32, 1), value
            )
    width = CT + 1
    sweep(start, start, middle, width, SEAM // 8, [PAD] * width, 2, 1, UNROLL_SEAM, True)
    still(middle, start, width, slice(PAD, PAD + SEAM))
    sweep(middle, start, end, width, SEAM // 8, [PAD] * width, 2, 1, UNROLL_SEAM, True)
    lane = lax.broadcasted_iota(jnp.int32, (4, TILE), 1)
    for t in range(RT * CT):
        r, c = t // CT, t % CT
        for place, row in ((0, 16 if c == 0 else 32), (4, 28 if c == 0 else 4)):
            rows = slice(PAD + row, PAD + row + 4)
            for f in range(3):
                ends = end[f, CT, rows, :]
                low = pltpu.roll(ends, 112 if r == 0 else 96, 1)
                high = pltpu.roll(ends, 96 if r == 0 else 120, 1)
                value = jnp.where(lane < REACH, low, end[f, r, rows, :])
                fixes[t, f, place : place + 4, :] = jnp.where(lane >= TILE - REACH, high, value)


def pack_kernel(lists, kept, inner, outer, packed, board):
    lists = Lists(lists)
    board[...] = jnp.zeros_like(board)
    far = jnp.int32(0)
    near = jnp.int32(0)
    for s in range(SLOTS):
        entry = lists.listed[s]
        own, _ = lists.inside(entry)
        foreign = (entry >= 0) & jnp.logical_not(own)
        top = lax.rem(lax.div(jnp.maximum(entry, 0), lists.span), RT) == 0
        here = jnp.minimum(near, MOVED - 1)
        there = jnp.minimum(far, MOVED - 1)
        near = near + own.astype(jnp.int32)
        far = far + foreign.astype(jnp.int32)

        @pl.when(own)
        def _(s=s, here=here):
            packed[s] = kept[here]

        @pl.when(foreign)
        def _(s=s, there=there, top=top):
            def cell(f, b):
                high = jnp.where(top, b - OUTER, b)
                low = jnp.where(top, b, b - INNER)
                high = pl.multiple_of(jnp.clip(high, 0, INNER - 8), 8)
                low = pl.multiple_of(jnp.clip(low, 0, OUTER - 8), 8)
                within = jnp.where(top, b >= OUTER, b < INNER)
                return jnp.where(
                    within, inner[there, f, pl.ds(high, 8), :], outer[there, f, pl.ds(low, 8), :]
                )

            def store(f, b, value):
                packed[s, f, b : b + 8, :] = value

            overlay(cell, lambda f: outer[there, f, OUTER : OUTER + 8, :], board, store)

        @pl.when(entry < 0)
        def _(s=s):
            packed[s] = jnp.zeros((3, TILE, TILE), jnp.float32)


def passed_along(block, distance):
    count = lax.axis_size("rows")
    return lax.ppermute(block, "rows", [((i - distance) % count, i) for i in range(count)])


def swapped(block):
    return lax.ppermute(block, "cols", [(0, 1), (1, 0)])


def scratch(*shape):
    return pltpu.VMEM(shape, jnp.float32)


def shards(depth, velocity, bed, slots):
    count = lax.axis_size("rows")
    half = count // 2
    listed = slots[0, 0]
    partner = passed_along(listed, half)
    state, turned = call(
        load_kernel,
        [HBM] * 3,
        [f32(4, CT, ROWS, TILE), f32(4, 32, ROWS)],
        [
            scratch(ROWS, COLS),
            scratch(2, ROWS, COLS),
            scratch(ROWS, COLS),
            pltpu.SemaphoreType.DMA((3,)),
        ],
    )(depth, velocity, bed)
    lists = jnp.concatenate([listed, partner])
    own, beside = call(edge_kernel, [SMEM, VMEM, VMEM], [f32(24, COLS), f32(48, COLS)])(
        lists, state, turned
    )
    other = swapped(beside)
    (wide,) = call(wide_kernel, [VMEM, VMEM], [f32(24, 2 * COLS)])(own, other)
    route = [(2 * r, 2 * r - 1) for r in range(1, count)]
    route += [(2 * r + 1, 2 * r + 2) for r in range(count - 1)]
    came = lax.ppermute(wide, ("rows", "cols"), route)
    pair = [scratch(3, MOVED, SPAN, TILE)] * 2
    gathered = [scratch(5, MOVED, SPAN, TILE)]
    (inner,) = call(
        inner_kernel, [SMEM, VMEM], [f32(MOVED, 3, INNER, TILE)], gathered + pair
    )(lists, state)
    far_inner = passed_along(inner, half)
    near = swapped(came)
    (fixes,) = call(
        seam_kernel,
        [SMEM] + [VMEM] * 4,
        [f32(RT * CT, 3, 8, TILE)],
        [scratch(5, CT + 1, SEAM_DEEP, TILE)]
        + [scratch(3, CT + 1, SEAM_DEEP, TILE)] * 2
        + [scratch(40, TILE)] * 3
        + [scratch(TILE, TILE)],
    )(lists, turned, other, came, near)
    (outer,) = call(
        outer_kernel, [SMEM] + [VMEM] * 4, [f32(MOVED, 3, OUTER + 8, TILE)], gathered + pair
    )(lists, state, came, near, fixes)
    far_outer = passed_along(outer, half)
    (kept,) = call(
        keep_kernel,
        [SMEM] + [VMEM] * 4,
        [f32(MOVED, 3, TILE, TILE)],
        gathered + pair + [scratch(TILE, TILE)],
    )(lists, state, came, near, fixes)
    (packed,) = call(
        pack_kernel, [SMEM] + [VMEM] * 3, [f32(SLOTS, 3, TILE, TILE)], [scratch(TILE, TILE)]
    )(lists, kept, far_inner, far_outer)
    return packed[None, None]


def solution(mesh):
    in_specs = (
        P(("groups", "rows"), "cols"),
        P(None, ("groups", "rows"), "cols"),
        P(("groups", "rows"), "cols"),
        P(("groups", "rows"), "cols", None),
    )
    out_specs = P(("groups", "rows"), "cols", None, None, None, None)

    return jax.shard_map(shards, mesh=mesh, in_specs=in_specs, out_specs=out_specs, check_vma=False)
```

```python
import jax
import jax.numpy as jnp
from jax import lax
from jax.experimental import pallas as pl
from jax.experimental.pallas import tpu as pltpu
from jax.sharding import PartitionSpec as P


TILE = 128
RT = 2
CT = 2
SLOTS = 3
MOVED = RT * CT // 2
ROWS = RT * TILE
COLS = CT * TILE
PAD = 16
SEAM = 40
SEAM_DEEP = SEAM + 2 * PAD
SPAN = TILE + 2 * PAD
INNER = 80
OUTER = TILE - INNER
REACH = 4
UNROLL_INNER = 3
UNROLL_OUTER = 2
UNROLL_FULL = 3
UNROLL_SEAM = 1

GRAVITY = 9.81
TIME_STEP = 0.04
DRY_DEPTH = 0.05
SPEED_FLOOR = 0.5
ROOT_GRAVITY = GRAVITY**0.5
TINY = 1.2e-38

VMEM = pl.BlockSpec(memory_space=pltpu.VMEM)
HBM = pl.BlockSpec(memory_space=pltpu.HBM)
SMEM = pl.BlockSpec(memory_space=pltpu.SMEM)


def f32(*shape):
    return jax.ShapeDtypeStruct(shape, jnp.float32)


def call(kernel, ins, outs, scratch=(), out_specs=None, aliases=None):
    return pl.pallas_call(
        kernel,
        in_specs=list(ins),
        out_specs=out_specs or tuple(SMEM if o.dtype == jnp.int32 else VMEM for o in outs),
        input_output_aliases=aliases or {},
        out_shape=tuple(outs),
        scratch_shapes=list(scratch),
        compiler_params=pltpu.CompilerParams(vmem_limit_bytes=20 * 2**20),
    )


def limited(down, up):
    return 0.5 * jnp.maximum(jnp.minimum(down, jnp.maximum(up, 0.0)), jnp.minimum(up, 0.0))


def speeds(water, normal, across):
    square = water * water
    factor = (water + water) / (square + jnp.maximum(square, DRY_DEPTH * DRY_DEPTH))
    return factor * normal, factor * across


def wave_speed(level):
    return (ROOT_GRAVITY * level) * lax.rsqrt(jnp.maximum(level, TINY))


def face_flux(left, right):
    water_l, speed_l, drift_l, ground_l = left
    water_r, speed_r, drift_r, ground_r = right
    top = jnp.maximum(ground_l, ground_r)
    level_l = jnp.maximum(water_l + (ground_l - top), 0.0)
    level_r = jnp.maximum(water_r + (ground_r - top), 0.0)
    wave_l = wave_speed(level_l)
    wave_r = wave_speed(level_r)
    lower = jnp.minimum(jnp.minimum(speed_l - wave_l, speed_r - wave_r), 0.0)
    upper = jnp.maximum(jnp.maximum(speed_l + wave_l, speed_r + wave_r), 0.0)
    inverse = 1.0 / jnp.maximum(upper - lower, SPEED_FLOOR)
    up = upper * inverse
    low = lower * inverse
    both = upper * low
    part_l = level_l * (up * speed_l - both)
    part_r = level_r * (both - low * speed_r)
    press_l = (0.5 * GRAVITY) * (level_l * level_l)
    press_r = (0.5 * GRAVITY) * (level_r * level_r)
    mass = part_l + part_r
    push = part_l * speed_l + part_r * speed_r + up * press_l - low * press_r
    side = part_l * drift_l + part_r * drift_r
    return mass, push - press_l, push - press_r, side


def sweep(src, ground, dst, width, steps, starts, lane_flow, row_flow, unroll, flush):
    sub = lax.broadcasted_iota(jnp.int32, (8, 128), 0)
    cols = range(width)

    def step(i, carry):
        shift = pl.multiple_of(i * 8, 8)

        def read(f, w, offset):
            held = src if f < 3 else ground
            return held[f, w, pl.ds(shift + starts[w] + offset, 8), :]

        now = []
        for w in cols:
            x = [read(f, w, 0) for f in range(4)]
            low, high, half = [], [], []
            for f in (0, lane_flow, row_flow, 3):
                down = x[f] - pltpu.roll(x[f], 1, 1)
                hs = limited(down, pltpu.roll(down, TILE - 1, 1))
                low.append(x[f] - hs)
                high.append(x[f] + hs)
                half.append(hs)
            fast = speeds(high[0], high[1], high[2])
            slow = speeds(low[0], low[1], low[2])
            left = [pltpu.roll(v, 1, 1) for v in (high[0], fast[0], fast[1], high[3])]
            mass, push_l, push_r, side = face_flux(left, (low[0], slow[0], slow[1], low[3]))
            weight = (2.0 * GRAVITY) * x[0]
            gain_water = mass - pltpu.roll(mass, TILE - 1, 1)
            gain_lane = push_r - pltpu.roll(push_l, TILE - 1, 1) - weight * (half[0] + half[3])
            gain_row = side - pltpu.roll(side, TILE - 1, 1)
            low, high, half = [], [], []
            for f in (0, row_flow, lane_flow, 3):
                hs = limited(x[f] - read(f, w, -1), read(f, w, 1) - x[f])
                low.append(x[f] - hs)
                high.append(x[f] + hs)
                half.append(hs)
            fast = speeds(high[0], high[1], high[2])
            slow = speeds(low[0], low[1], low[2])
            old_high, old_flux, old_gain = carry[w]
            high_now = tuple(pltpu.roll(v, 1, 0) for v in (high[0], fast[0], fast[1], high[3]))
            left = [jnp.where(sub == 0, o, n) for o, n in zip(old_high, high_now)]
            mass, push_l, push_r, side = face_flux(left, (low[0], slow[0], slow[1], low[3]))
            gain = (
                gain_water + mass,
                gain_lane + side,
                gain_row + push_r - weight * (half[0] + half[3]),
            )
            flux_now = tuple(pltpu.roll(v, 7, 0) for v in (mass, side, push_l))
            for f, g, o, n in zip((0, lane_flow, row_flow), old_gain, old_flux, flux_now):
                dst[f, w, pl.ds(shift + starts[w] - 8, 8), :] = read(f, w, -8) + TIME_STEP * (
                    g - jnp.where(sub == 7, n, o)
                )
            now.append((high_now, flux_now, gain))
        return tuple(now)

    zero = jnp.zeros((8, 128), jnp.float32)
    start = tuple(((zero,) * 4, (zero,) * 3, (zero,) * 3) for _ in cols)
    carry = lax.fori_loop(0, steps, step, start, unroll=unroll)
    if flush:
        for w in cols:
            rows = pl.ds(starts[w] + 8 * (steps - 1), 8)
            _, old_flux, old_gain = carry[w]
            for f, g, o in zip((0, lane_flow, row_flow), old_gain, old_flux):
                dst[f, w, rows, :] = src[f, w, rows, :] + TIME_STEP * (g - o)


def load_kernel(listed, depth, velocity, bed, state, turned, again, water, speed, ground, sems):
    copies = [
        pltpu.make_async_copy(depth, water, sems.at[0]),
        pltpu.make_async_copy(velocity, speed, sems.at[1]),
        pltpu.make_async_copy(bed, ground, sems.at[2]),
    ]
    for copy in copies:
        copy.start()
    for k in range(SLOTS):
        again[k] = listed[k]
    for copy in copies:
        copy.wait()
    for w in range(CT):
        cols = slice(w * TILE, (w + 1) * TILE)
        for r in range(0, ROWS, 8):
            rows = slice(r, r + 8)
            here = water[rows, cols]
            state[0, w, rows, :] = here
            state[1, w, rows, :] = here * speed[0, rows, cols]
            state[2, w, rows, :] = here * speed[1, rows, cols]
            state[3, w, rows, :] = ground[rows, cols]
    lane = lax.broadcasted_iota(jnp.int32, (TILE, TILE), 1)
    for f in range(4):
        for r in range(RT):
            held = slice(r * TILE, (r + 1) * TILE)
            one, two = state[f, 0, held, :], state[f, CT - 1, held, :]
            flipped = jnp.where(lane < TILE // 2, one, two).T
            turned[f, 0:8, held] = flipped[TILE - 8 :, :]
            turned[f, 8:16, held] = flipped[:8, :]
            flipped = jnp.where(lane < TILE // 2, two, one).T
            turned[f, 16:24, held] = flipped[TILE - 8 :, :]
            turned[f, 24:32, held] = flipped[:8, :]


class Lists:
    def __init__(self, lists):
        self.rows = lax.axis_index("rows")
        self.cols = lax.axis_index("cols")
        self.span = CT * lax.axis_size("cols")
        self.ids = [
            (self.rows * RT + t // CT) * self.span + self.cols * CT + t % CT for t in range(RT * CT)
        ]
        self.listed = [lists[k] for k in range(SLOTS)]
        self.partner = [lists[SLOTS + k] for k in range(SLOTS)]

    def inside(self, entry):
        found = [entry == i for i in self.ids]
        any_found = found[0]
        local = jnp.int32(0)
        for t in range(1, RT * CT):
            any_found = any_found | found[t]
            local = jnp.where(found[t], jnp.int32(t), local)
        return any_found, local

    def active(self, t):
        hit = self.listed[0] == self.ids[t]
        for entry in self.listed[1:] + self.partner:
            hit = hit | (entry == self.ids[t])
        return hit

    def flags(self):
        return [jnp.where(self.active(t), 1.0, 0.0) for t in range(RT * CT)]

    def outgoing(self):
        used = [jnp.bool_(False)] * MOVED
        tile = [jnp.int32(0)] * MOVED
        rank = jnp.int32(0)
        for entry in self.partner:
            own, local = self.inside(entry)
            for k in range(MOVED):
                take = own & (rank == k)
                used[k] = used[k] | take
                tile[k] = jnp.where(take, local, tile[k])
            rank = rank + own.astype(jnp.int32)
        return used, tile

    def kept(self):
        used = [jnp.bool_(False)] * MOVED
        tile = [jnp.int32(0)] * MOVED
        rank = jnp.int32(0)
        for entry in self.listed:
            own, local = self.inside(entry)
            for k in range(MOVED):
                take = own & (rank == k)
                used[k] = used[k] | take
                tile[k] = jnp.where(take, local, tile[k])
            rank = rank + own.astype(jnp.int32)
        return used, tile


def edge_kernel(lists, state, turned, own, out):
    lists = Lists(lists)
    is_left = lists.cols == 0
    flags = lists.flags()
    for w in range(CT):
        cols = slice(w * TILE, (w + 1) * TILE)
        for f in range(4):
            rows = slice(4 * f, 4 * f + 4)
            first = state[f, w, 0:REACH, :]
            last = state[f, w, ROWS - REACH : ROWS, :]
            own[rows, cols] = jnp.where(is_left, first, last)
            out[rows, cols] = jnp.where(is_left, last, first)
        first, last = flags[w], flags[(RT - 1) * CT + w]
        own[16:24, cols] = jnp.full((8, TILE), jnp.where(is_left, first, last), jnp.float32)
        out[16:24, cols] = jnp.full((8, TILE), jnp.where(is_left, last, first), jnp.float32)
    for f in range(4):
        rows = slice(24 + 4 * f, 28 + 4 * f)
        out[rows, :] = jnp.where(is_left, turned[f, 4:8, :], turned[f, 8:12, :])
    for r in range(RT):
        flag = jnp.where(is_left, flags[r * CT + CT - 1], flags[r * CT])
        out[40:48, r * TILE : (r + 1) * TILE] = jnp.full((8, TILE), flag, jnp.float32)


def wide_kernel(own, other, out):
    is_left = lax.axis_index("cols") == 0
    near = other[0:24, :]
    out[:, 0:COLS] = jnp.where(is_left, own[...], near)
    out[:, COLS : 2 * COLS] = jnp.where(is_left, near, own[...])


def halo_pieces(came, near, f, upper):
    is_left = lax.axis_index("cols") == 0
    rows = slice(4 * f, 4 * f + 4)
    halo = jnp.where(is_left == upper, came[rows, :], near[rows, :])
    part = [halo[:, q * TILE : (q + 1) * TILE] for q in range(2 * CT)]
    return (
        jnp.where(is_left, part[0], part[2]),
        jnp.where(is_left, part[1], part[3]),
        jnp.where(is_left, part[2], part[1]),
    )


def gather_pair(tile, flags, state, start, halos):
    blank = jnp.zeros((4, TILE), jnp.float32)
    over = slice(PAD - 8, PAD)
    under = slice(PAD + TILE, PAD + TILE + 8)
    for k in range(MOVED):
        r, c = tile[k] // CT, tile[k] % CT
        base = pl.multiple_of(r * TILE, TILE)
        for f in range(4):
            start[f, k, PAD : PAD + TILE, :] = state[f, c, pl.ds(base, TILE), :]
        if halos is not None:
            ends = [
                [jnp.where(c == 0, *halo_pieces(*halos, f, upper)[:2]) for f in range(5)]
                for upper in (True, False)
            ]

        @pl.when(r == 0)
        def _(k=k, c=c):
            for f in range(4):
                start[f, k, under, :] = state[f, c, TILE : TILE + 8, :]
            flag = jnp.where(c == 0, flags[CT], flags[CT + 1])
            start[4, k, under, :] = jnp.full((8, TILE), flag, jnp.float32)
            if halos is not None:
                for f in range(5):
                    start[f, k, PAD - 8 : PAD - 4, :] = blank
                    start[f, k, PAD - 4 : PAD, :] = ends[0][f]

        @pl.when(r == RT - 1)
        def _(k=k, c=c):
            for f in range(4):
                start[f, k, over, :] = state[f, c, TILE - 8 : TILE, :]
            flag = jnp.where(c == 0, flags[0], flags[1])
            start[4, k, over, :] = jnp.full((8, TILE), flag, jnp.float32)
            if halos is not None:
                for f in range(5):
                    start[f, k, PAD + TILE : PAD + TILE + 4, :] = ends[1][f]
                    start[f, k, PAD + TILE + 4 : PAD + TILE + 8, :] = blank


def still(dst, src, width, rows):
    for w in range(width):
        alive = src[4, w, rows, :] > 0.5
        for f in range(3):
            dst[f, w, rows, :] = jnp.where(alive, dst[f, w, rows, :], src[f, w, rows, :])


def aligned(row):
    return row if isinstance(row, int) else pl.multiple_of(row, 8)


def advance_pair(start, middle, end, firsts, count, masked, unroll):
    steps = count // 8 + 2
    starts = [aligned(first) + (PAD - 8) for first in firsts]
    sweep(start, start, middle, MOVED, steps, starts, 1, 2, unroll, True)
    for w in range(MOVED):
        for row in masked[w]:
            rows = pl.ds(aligned(row) + PAD, 8)
            alive = start[4, w, rows, :] > 0.5
            for f in range(3):
                middle[f, w, rows, :] = jnp.where(alive, middle[f, w, rows, :], start[f, w, rows, :])
    sweep(middle, start, end, MOVED, steps, starts, 1, 2, unroll, False)


def overlay(cell, fix, board, store):
    lane = lax.broadcasted_iota(jnp.int32, (8, TILE), 1)
    for f in range(3):
        board[8 * f : 8 * f + 8, :] = fix(f)
    turned = board[...].T
    for f in range(3):
        for b in range(0, TILE, 8):
            strip = turned[b : b + 8, :]
            left = pltpu.roll(strip, (TILE - 8 * f) % TILE, 1)
            right = pltpu.roll(strip, TILE - 8 - 8 * f, 1)
            value = jnp.where(lane < REACH, left, cell(f, b))
            store(f, b, jnp.where(lane >= TILE - REACH, right, value))


def inner_kernel(lists, state, out, start, middle, end):
    lists = Lists(lists)
    _, tile = lists.outgoing()
    gather_pair(tile, lists.flags(), state, start, None)
    top = [t // CT == 0 for t in tile]
    firsts = [jnp.where(u, OUTER, 0) for u in top]
    masked = [[jnp.where(u, TILE, -8)] for u in top]
    advance_pair(start, middle, end, firsts, INNER, masked, UNROLL_INNER)
    for k in range(MOVED):
        rows = pl.ds(pl.multiple_of(firsts[k], 8) + PAD, INNER)
        for f in range(3):
            out[k, f] = end[f, k, rows, :]


def outer_kernel(lists, state, came, near, fixes, out, start, middle, end):
    lists = Lists(lists)
    _, tile = lists.outgoing()
    gather_pair(tile, lists.flags(), state, start, (came, near))
    top = [t // CT == 0 for t in tile]
    firsts = [jnp.where(u, 0, INNER) for u in top]
    masked = [[jnp.where(u, -8, TILE)] for u in top]
    advance_pair(start, middle, end, firsts, OUTER, masked, UNROLL_OUTER)
    for k in range(MOVED):
        rows = pl.ds(pl.multiple_of(firsts[k], 8) + PAD, OUTER)
        for f in range(3):
            out[k, f, 0:OUTER, :] = end[f, k, rows, :]
            out[k, f, OUTER : OUTER + 8, :] = fixes[tile[k], f]


def keep_kernel(lists, state, came, near, fixes, packed, out, start, middle, end, board, sems):
    lists = Lists(lists)
    used, tile = lists.kept()

    @pl.when(used[0])
    def _():
        gather_pair(tile, lists.flags(), state, start, (came, near))
        masked = [[-8, TILE]] * MOVED
        advance_pair(start, middle, end, [0] * MOVED, TILE, masked, UNROLL_FULL)
        board[...] = jnp.zeros_like(board)
        for k in range(MOVED):

            def store(f, b, value, k=k):
                out[k, f, b : b + 8, :] = value

            overlay(
                lambda f, b, k=k: end[f, k, PAD + b : PAD + b + 8, :],
                lambda f, k=k: fixes[tile[k], f],
                board,
                store,
            )

    out[MOVED] = jnp.zeros((3, TILE, TILE), jnp.float32)
    copies = []
    rank = jnp.int32(0)
    for s in range(SLOTS):
        entry = lists.listed[s]
        own, _ = lists.inside(entry)
        place = jnp.where(own, jnp.minimum(rank, MOVED - 1), MOVED)
        rank = rank + own.astype(jnp.int32)
        copy = pltpu.make_async_copy(out.at[place], packed.at[s], sems.at[s])
        copies.append((own | (entry < 0), copy))
    for due, copy in copies:
        pl.when(due)(copy.start)
    for due, copy in copies:
        pl.when(due)(copy.wait)


def seam_kernel(lists, turned, other, came, near, fixes, start, middle, end, one, two, side, board):
    lists = Lists(lists)
    is_left = lists.cols == 0
    flags = lists.flags()
    lane = lax.broadcasted_iota(jnp.int32, (8, TILE), 1)
    for w in range(CT):
        cols = slice(w * TILE, (w + 1) * TILE)
        for f in range(5):
            beside = other[24 + 4 * f : 28 + 4 * f, cols]
            start[f, w, PAD + 8 : PAD + 12, :] = jnp.where(is_left, beside, 0.0)
            start[f, w, PAD + 12 : PAD + 16, :] = jnp.where(is_left, 0.0, beside)
            if f < 4:
                start[f, w, PAD : PAD + 8, :] = turned[f, 0:8, cols]
                start[f, w, PAD + 16 : PAD + 40, :] = turned[f, 8:32, cols]
        for row, c in ((0, CT - 1), (16, 0), (24, 0), (32, CT - 1)):
            full = jnp.full((8, TILE), flags[w * CT + c], jnp.float32)
            start[4, w, PAD + row : PAD + row + 8, :] = full
    for f in range(5):
        for place, upper in ((0, False), (4, True)):
            rows = slice(8 * f + place, 8 * f + place + 4)
            pieces = halo_pieces(came, near, f, upper)
            one[rows, :], two[rows, :], side[rows, :] = pieces
    board[...] = jnp.zeros_like(board)
    for b in range(0, 40, 8):
        rows = slice(b, b + 8)
        first, second, beside = one[rows, :], two[rows, :], side[rows, :]
        value = jnp.where(lane < 8, pltpu.roll(second, 8, 1), 0.0)
        value = jnp.where((lane >= 8) & (lane < 12) & is_left, pltpu.roll(beside, 8, 1), value)
        far = jnp.logical_not(is_left)
        value = jnp.where((lane >= 12) & (lane < 16) & far, pltpu.roll(beside, 16, 1), value)
        value = jnp.where((lane >= 16) & (lane < 24), pltpu.roll(first, 16, 1), value)
        value = jnp.where((lane >= 24) & (lane < 32), pltpu.roll(first, 32, 1), value)
        board[rows, :] = jnp.where((lane >= 32) & (lane < 40), pltpu.roll(second, 32, 1), value)
    turned = board[...].T
    for f in range(5):
        for b in range(0, SEAM, 8):
            rows = slice(PAD + b, PAD + b + 8)
            first, second = start[f, 0, rows, :], start[f, 1, rows, :]
            ends = pltpu.roll(turned[b : b + 8, :], (8 - 8 * f) % TILE, 1)
            value = jnp.where(lane < 8, pltpu.roll(second, 8, 1), 0.0)
            value = jnp.where((lane >= 8) & (lane < 16), ends, value)
            value = jnp.where((lane >= 16) & (lane < 24), pltpu.roll(first, 16, 1), value)
            value = jnp.where((lane >= 24) & (lane < 32), pltpu.roll(first, 32, 1), value)
            start[f, CT, rows, :] = jnp.where(
                (lane >= 32) & (lane < 40), pltpu.roll(second, 32, 1), value
            )
    width = CT + 1
    sweep(start, start, middle, width, SEAM // 8, [PAD] * width, 2, 1, UNROLL_SEAM, True)
    still(middle, start, width, slice(PAD, PAD + SEAM))
    sweep(middle, start, end, width, SEAM // 8, [PAD] * width, 2, 1, UNROLL_SEAM, True)
    lane = lax.broadcasted_iota(jnp.int32, (4, TILE), 1)
    for t in range(RT * CT):
        r, c = t // CT, t % CT
        for place, row in ((0, 16 if c == 0 else 32), (4, 28 if c == 0 else 4)):
            rows = slice(PAD + row, PAD + row + 4)
            for f in range(3):
                ends = end[f, CT, rows, :]
                low = pltpu.roll(ends, 112 if r == 0 else 96, 1)
                high = pltpu.roll(ends, 96 if r == 0 else 120, 1)
                value = jnp.where(lane < REACH, low, end[f, r, rows, :])
                fixes[t, f, place : place + 4, :] = jnp.where(lane >= TILE - REACH, high, value)


def pack_kernel(lists, inner, outer, before, packed, staged, board, sems):
    del before
    lists = Lists(lists)
    board[...] = jnp.zeros_like(board)
    rank = jnp.int32(0)
    copies = []
    for s in range(SLOTS):
        entry = lists.listed[s]
        own, _ = lists.inside(entry)
        foreign = (entry >= 0) & jnp.logical_not(own)
        top = lax.rem(lax.div(jnp.maximum(entry, 0), lists.span), RT) == 0
        there = jnp.minimum(rank, MOVED - 1)
        rank = rank + foreign.astype(jnp.int32)
        parts = [
            pltpu.make_async_copy(staged.at[s, f], packed.at[s, f], sems.at[s, f]) for f in range(3)
        ]
        copies.append((foreign, parts))

        @pl.when(foreign)
        def _(s=s, there=there, top=top, parts=parts):
            def cell(f, b):
                high = jnp.where(top, b - OUTER, b)
                low = jnp.where(top, b, b - INNER)
                high = pl.multiple_of(jnp.clip(high, 0, INNER - 8), 8)
                low = pl.multiple_of(jnp.clip(low, 0, OUTER - 8), 8)
                within = jnp.where(top, b >= OUTER, b < INNER)
                return jnp.where(
                    within, inner[there, f, pl.ds(high, 8), :], outer[there, f, pl.ds(low, 8), :]
                )

            def store(f, b, value):
                staged[s, f, b : b + 8, :] = value
                if b == TILE - 8:
                    parts[f].start()

            overlay(cell, lambda f: outer[there, f, OUTER : OUTER + 8, :], board, store)

    for foreign, parts in copies:

        @pl.when(foreign)
        def _(parts=parts):
            for part in parts:
                part.wait()


def passed_along(block, distance):
    count = lax.axis_size("rows")
    return lax.ppermute(block, "rows", [((i - distance) % count, i) for i in range(count)])


def swapped(block):
    return lax.ppermute(block, "cols", [(0, 1), (1, 0)])


def in_hbm(block):
    return pltpu.with_memory_space_constraint(block, pltpu.HBM)


def scratch(*shape):
    return pltpu.VMEM(shape, jnp.float32)


def shards(depth, velocity, bed, slots):
    count = lax.axis_size("rows")
    half = count // 2
    listed = slots[0, 0]
    partner = passed_along(slots, half)[0, 0]
    state, turned, again = call(
        load_kernel,
        [SMEM] + [HBM] * 3,
        [
            f32(4, CT, ROWS, TILE),
            f32(4, 32, ROWS),
            jax.ShapeDtypeStruct((SLOTS,), jnp.int32),
        ],
        [
            scratch(ROWS, COLS),
            scratch(2, ROWS, COLS),
            scratch(ROWS, COLS),
            pltpu.SemaphoreType.DMA((3,)),
        ],
    )(*[in_hbm(v) for v in (listed, depth, velocity, bed)])
    lists = jnp.concatenate([again, partner])
    own, beside = call(edge_kernel, [SMEM, VMEM, VMEM], [f32(24, COLS), f32(48, COLS)])(
        lists, state, turned
    )
    other = swapped(beside)
    (wide,) = call(wide_kernel, [VMEM, VMEM], [f32(24, 2 * COLS)])(own, other)
    route = [(2 * r, 2 * r - 1) for r in range(1, count)]
    route += [(2 * r + 1, 2 * r + 2) for r in range(count - 1)]
    came = lax.ppermute(wide, ("rows", "cols"), route)
    pair = [scratch(3, MOVED, SPAN, TILE)] * 2
    gathered = [scratch(5, MOVED, SPAN, TILE)]
    (inner,) = call(
        inner_kernel, [SMEM, VMEM], [f32(MOVED, 3, INNER, TILE)], gathered + pair
    )(lists, state)
    far_inner = passed_along(inner, half)
    near = swapped(came)
    (fixes,) = call(
        seam_kernel,
        [SMEM] + [VMEM] * 4,
        [f32(RT * CT, 3, 8, TILE)],
        [scratch(5, CT + 1, SEAM_DEEP, TILE)]
        + [scratch(3, CT + 1, SEAM_DEEP, TILE)] * 2
        + [scratch(40, TILE)] * 3
        + [scratch(TILE, TILE)],
    )(lists, turned, other, came, near)
    (outer,) = call(
        outer_kernel, [SMEM] + [VMEM] * 4, [f32(MOVED, 3, OUTER + 8, TILE)], gathered + pair
    )(lists, state, came, near, fixes)
    far_outer = passed_along(outer, half)
    place = f32(SLOTS, 3, TILE, TILE)
    (packed,) = call(
        keep_kernel,
        [SMEM] + [VMEM] * 4,
        [place],
        [scratch(MOVED + 1, 3, TILE, TILE)]
        + gathered
        + pair
        + [scratch(TILE, TILE), pltpu.SemaphoreType.DMA((SLOTS,))],
        (HBM,),
    )(lists, state, came, near, fixes)
    (packed,) = call(
        pack_kernel,
        [SMEM] + [VMEM] * 2 + [HBM],
        [place],
        [
            scratch(SLOTS, 3, TILE, TILE),
            scratch(TILE, TILE),
            pltpu.SemaphoreType.DMA((SLOTS, 3)),
        ],
        (HBM,),
        {3: 0},
    )(lists, far_inner, far_outer, packed)
    return packed[None, None]


def solution(mesh):
    in_specs = (
        P(("groups", "rows"), "cols"),
        P(None, ("groups", "rows"), "cols"),
        P(("groups", "rows"), "cols"),
        P(("groups", "rows"), "cols", None),
    )
    out_specs = P(("groups", "rows"), "cols", None, None, None, None)

    return jax.shard_map(shards, mesh=mesh, in_specs=in_specs, out_specs=out_specs, check_vma=False)
```

```python
import jax
import jax.numpy as jnp
from jax import lax
from jax.experimental import pallas as pl
from jax.experimental.pallas import tpu as pltpu
from jax.sharding import PartitionSpec as P


TILE = 128
RT = 2
CT = 2
SLOTS = 3
MOVED = RT * CT // 2
ROWS = RT * TILE
COLS = CT * TILE
PAD = 16
SEAM = 40
SEAM_DEEP = SEAM + 2 * PAD
SPAN = TILE + 2 * PAD
INNER = 80
OUTER = TILE - INNER
REACH = 4
UNROLL_INNER = 6
UNROLL_OUTER = 8
UNROLL_FULL = 6
UNROLL_SEAM = 5

GRAVITY = 9.81
TIME_STEP = 0.04
DRY_DEPTH = 0.05
SPEED_FLOOR = 0.5
ROOT_GRAVITY = GRAVITY**0.5
TINY = 1.2e-38

VMEM = pl.BlockSpec(memory_space=pltpu.VMEM)
HBM = pl.BlockSpec(memory_space=pltpu.HBM)
SMEM = pl.BlockSpec(memory_space=pltpu.SMEM)


def f32(*shape):
    return jax.ShapeDtypeStruct(shape, jnp.float32)


def call(kernel, ins, outs, scratch=(), out_specs=None, aliases=None):
    return pl.pallas_call(
        kernel,
        in_specs=list(ins),
        out_specs=out_specs or tuple(SMEM if o.dtype == jnp.int32 else VMEM for o in outs),
        input_output_aliases=aliases or {},
        out_shape=tuple(outs),
        scratch_shapes=list(scratch),
        compiler_params=pltpu.CompilerParams(vmem_limit_bytes=20 * 2**20),
    )


def limited(down, up):
    return 0.5 * jnp.maximum(jnp.minimum(down, jnp.maximum(up, 0.0)), jnp.minimum(up, 0.0))


def speeds(water, normal, across):
    square = water * water
    factor = (water + water) / (square + jnp.maximum(square, DRY_DEPTH * DRY_DEPTH))
    return factor * normal, factor * across


def wave_speed(level):
    return (ROOT_GRAVITY * level) * lax.rsqrt(jnp.maximum(level, TINY))


def face_flux(left, right):
    water_l, speed_l, drift_l, ground_l = left
    water_r, speed_r, drift_r, ground_r = right
    top = jnp.maximum(ground_l, ground_r)
    level_l = jnp.maximum(water_l + (ground_l - top), 0.0)
    level_r = jnp.maximum(water_r + (ground_r - top), 0.0)
    wave_l = wave_speed(level_l)
    wave_r = wave_speed(level_r)
    lower = jnp.minimum(jnp.minimum(speed_l - wave_l, speed_r - wave_r), 0.0)
    upper = jnp.maximum(jnp.maximum(speed_l + wave_l, speed_r + wave_r), 0.0)
    inverse = 1.0 / jnp.maximum(upper - lower, SPEED_FLOOR)
    up = upper * inverse
    low = lower * inverse
    both = upper * low
    part_l = level_l * (up * speed_l - both)
    part_r = level_r * (both - low * speed_r)
    press_l = (0.5 * GRAVITY) * (level_l * level_l)
    press_r = (0.5 * GRAVITY) * (level_r * level_r)
    mass = part_l + part_r
    push = part_l * speed_l + part_r * speed_r + up * press_l - low * press_r
    side = part_l * drift_l + part_r * drift_r
    return mass, push - press_l, push - press_r, side


def sweep(src, ground, dst, width, steps, starts, lane_flow, row_flow, unroll, flush):
    sub = lax.broadcasted_iota(jnp.int32, (8, 128), 0)
    cols = range(width)

    def step(i, carry):
        shift = pl.multiple_of(i * 8, 8)

        def read(f, w, offset):
            held = src if f < 3 else ground
            return held[f, w, pl.ds(shift + starts[w] + offset, 8), :]

        now = []
        for w in cols:
            x = [read(f, w, 0) for f in range(4)]
            low, high, half = [], [], []
            for f in (0, lane_flow, row_flow, 3):
                down = x[f] - pltpu.roll(x[f], 1, 1)
                hs = limited(down, pltpu.roll(down, TILE - 1, 1))
                low.append(x[f] - hs)
                high.append(x[f] + hs)
                half.append(hs)
            fast = speeds(high[0], high[1], high[2])
            slow = speeds(low[0], low[1], low[2])
            left = [pltpu.roll(v, 1, 1) for v in (high[0], fast[0], fast[1], high[3])]
            mass, push_l, push_r, side = face_flux(left, (low[0], slow[0], slow[1], low[3]))
            weight = (2.0 * GRAVITY) * x[0]
            gain_water = mass - pltpu.roll(mass, TILE - 1, 1)
            gain_lane = push_r - pltpu.roll(push_l, TILE - 1, 1) - weight * (half[0] + half[3])
            gain_row = side - pltpu.roll(side, TILE - 1, 1)
            low, high, half = [], [], []
            for f in (0, row_flow, lane_flow, 3):
                hs = limited(x[f] - read(f, w, -1), read(f, w, 1) - x[f])
                low.append(x[f] - hs)
                high.append(x[f] + hs)
                half.append(hs)
            fast = speeds(high[0], high[1], high[2])
            slow = speeds(low[0], low[1], low[2])
            old_high, old_flux, old_gain = carry[w]
            high_now = tuple(pltpu.roll(v, 1, 0) for v in (high[0], fast[0], fast[1], high[3]))
            left = [jnp.where(sub == 0, o, n) for o, n in zip(old_high, high_now)]
            mass, push_l, push_r, side = face_flux(left, (low[0], slow[0], slow[1], low[3]))
            gain = (
                gain_water + mass,
                gain_lane + side,
                gain_row + push_r - weight * (half[0] + half[3]),
            )
            flux_now = tuple(pltpu.roll(v, 7, 0) for v in (mass, side, push_l))
            for f, g, o, n in zip((0, lane_flow, row_flow), old_gain, old_flux, flux_now):
                dst[f, w, pl.ds(shift + starts[w] - 8, 8), :] = read(f, w, -8) + TIME_STEP * (
                    g - jnp.where(sub == 7, n, o)
                )
            now.append((high_now, flux_now, gain))
        return tuple(now)

    zero = jnp.zeros((8, 128), jnp.float32)
    start = tuple(((zero,) * 4, (zero,) * 3, (zero,) * 3) for _ in cols)
    carry = lax.fori_loop(0, steps, step, start, unroll=unroll)
    if flush:
        for w in cols:
            rows = pl.ds(starts[w] + 8 * (steps - 1), 8)
            _, old_flux, old_gain = carry[w]
            for f, g, o in zip((0, lane_flow, row_flow), old_gain, old_flux):
                dst[f, w, rows, :] = src[f, w, rows, :] + TIME_STEP * (g - o)


def load_kernel(listed, depth, velocity, bed, state, turned, again, water, speed, ground, sems):
    copies = [
        pltpu.make_async_copy(depth, water, sems.at[0]),
        pltpu.make_async_copy(velocity, speed, sems.at[1]),
        pltpu.make_async_copy(bed, ground, sems.at[2]),
    ]
    for copy in copies:
        copy.start()
    for k in range(SLOTS):
        again[k] = listed[k]
    for copy in copies:
        copy.wait()
    for w in range(CT):
        cols = slice(w * TILE, (w + 1) * TILE)
        for r in range(0, ROWS, 8):
            rows = slice(r, r + 8)
            here = water[rows, cols]
            state[0, w, rows, :] = here
            state[1, w, rows, :] = here * speed[0, rows, cols]
            state[2, w, rows, :] = here * speed[1, rows, cols]
            state[3, w, rows, :] = ground[rows, cols]
    lane = lax.broadcasted_iota(jnp.int32, (TILE, TILE), 1)
    for f in range(4):
        for r in range(RT):
            held = slice(r * TILE, (r + 1) * TILE)
            one, two = state[f, 0, held, :], state[f, CT - 1, held, :]
            flipped = jnp.where(lane < TILE // 2, one, two).T
            turned[f, 0:8, held] = flipped[TILE - 8 :, :]
            turned[f, 8:16, held] = flipped[:8, :]
            flipped = jnp.where(lane < TILE // 2, two, one).T
            turned[f, 16:24, held] = flipped[TILE - 8 :, :]
            turned[f, 24:32, held] = flipped[:8, :]


class Lists:
    def __init__(self, lists):
        self.rows = lax.axis_index("rows")
        self.cols = lax.axis_index("cols")
        self.span = CT * lax.axis_size("cols")
        self.ids = [
            (self.rows * RT + t // CT) * self.span + self.cols * CT + t % CT for t in range(RT * CT)
        ]
        self.listed = [lists[k] for k in range(SLOTS)]
        self.partner = [lists[SLOTS + k] for k in range(SLOTS)]

    def inside(self, entry):
        found = [entry == i for i in self.ids]
        any_found = found[0]
        local = jnp.int32(0)
        for t in range(1, RT * CT):
            any_found = any_found | found[t]
            local = jnp.where(found[t], jnp.int32(t), local)
        return any_found, local

    def active(self, t):
        hit = self.listed[0] == self.ids[t]
        for entry in self.listed[1:] + self.partner:
            hit = hit | (entry == self.ids[t])
        return hit

    def flags(self):
        return [jnp.where(self.active(t), 1.0, 0.0) for t in range(RT * CT)]

    def outgoing(self):
        used = [jnp.bool_(False)] * MOVED
        tile = [jnp.int32(0)] * MOVED
        rank = jnp.int32(0)
        for entry in self.partner:
            own, local = self.inside(entry)
            for k in range(MOVED):
                take = own & (rank == k)
                used[k] = used[k] | take
                tile[k] = jnp.where(take, local, tile[k])
            rank = rank + own.astype(jnp.int32)
        return used, tile

    def kept(self):
        used = [jnp.bool_(False)] * MOVED
        tile = [jnp.int32(0)] * MOVED
        rank = jnp.int32(0)
        for entry in self.listed:
            own, local = self.inside(entry)
            for k in range(MOVED):
                take = own & (rank == k)
                used[k] = used[k] | take
                tile[k] = jnp.where(take, local, tile[k])
            rank = rank + own.astype(jnp.int32)
        return used, tile


def edge_kernel(lists, state, turned, own, out):
    lists = Lists(lists)
    is_left = lists.cols == 0
    flags = lists.flags()
    for w in range(CT):
        cols = slice(w * TILE, (w + 1) * TILE)
        for f in range(4):
            rows = slice(4 * f, 4 * f + 4)
            first = state[f, w, 0:REACH, :]
            last = state[f, w, ROWS - REACH : ROWS, :]
            own[rows, cols] = jnp.where(is_left, first, last)
            out[rows, cols] = jnp.where(is_left, last, first)
        first, last = flags[w], flags[(RT - 1) * CT + w]
        own[16:24, cols] = jnp.full((8, TILE), jnp.where(is_left, first, last), jnp.float32)
        out[16:24, cols] = jnp.full((8, TILE), jnp.where(is_left, last, first), jnp.float32)
    for f in range(4):
        rows = slice(24 + 4 * f, 28 + 4 * f)
        out[rows, :] = jnp.where(is_left, turned[f, 4:8, :], turned[f, 8:12, :])
    for r in range(RT):
        flag = jnp.where(is_left, flags[r * CT + CT - 1], flags[r * CT])
        out[40:48, r * TILE : (r + 1) * TILE] = jnp.full((8, TILE), flag, jnp.float32)


def wide_kernel(own, other, out):
    is_left = lax.axis_index("cols") == 0
    near = other[0:24, :]
    out[:, 0:COLS] = jnp.where(is_left, own[...], near)
    out[:, COLS : 2 * COLS] = jnp.where(is_left, near, own[...])


def halo_pieces(came, near, f, upper):
    is_left = lax.axis_index("cols") == 0
    rows = slice(4 * f, 4 * f + 4)
    halo = jnp.where(is_left == upper, came[rows, :], near[rows, :])
    part = [halo[:, q * TILE : (q + 1) * TILE] for q in range(2 * CT)]
    return (
        jnp.where(is_left, part[0], part[2]),
        jnp.where(is_left, part[1], part[3]),
        jnp.where(is_left, part[2], part[1]),
    )


def gather_pair(tile, flags, state, start, halos):
    blank = jnp.zeros((4, TILE), jnp.float32)
    over = slice(PAD - 8, PAD)
    under = slice(PAD + TILE, PAD + TILE + 8)
    for k in range(MOVED):
        r, c = tile[k] // CT, tile[k] % CT
        base = pl.multiple_of(r * TILE, TILE)
        for f in range(4):
            start[f, k, PAD : PAD + TILE, :] = state[f, c, pl.ds(base, TILE), :]
        if halos is not None:
            ends = [
                [jnp.where(c == 0, *halo_pieces(*halos, f, upper)[:2]) for f in range(5)]
                for upper in (True, False)
            ]

        @pl.when(r == 0)
        def _(k=k, c=c):
            for f in range(4):
                start[f, k, under, :] = state[f, c, TILE : TILE + 8, :]
            flag = jnp.where(c == 0, flags[CT], flags[CT + 1])
            start[4, k, under, :] = jnp.full((8, TILE), flag, jnp.float32)
            if halos is not None:
                for f in range(5):
                    start[f, k, PAD - 8 : PAD - 4, :] = blank
                    start[f, k, PAD - 4 : PAD, :] = ends[0][f]

        @pl.when(r == RT - 1)
        def _(k=k, c=c):
            for f in range(4):
                start[f, k, over, :] = state[f, c, TILE - 8 : TILE, :]
            flag = jnp.where(c == 0, flags[0], flags[1])
            start[4, k, over, :] = jnp.full((8, TILE), flag, jnp.float32)
            if halos is not None:
                for f in range(5):
                    start[f, k, PAD + TILE : PAD + TILE + 4, :] = ends[1][f]
                    start[f, k, PAD + TILE + 4 : PAD + TILE + 8, :] = blank


def still(dst, src, width, rows):
    for w in range(width):
        alive = src[4, w, rows, :] > 0.5
        for f in range(3):
            dst[f, w, rows, :] = jnp.where(alive, dst[f, w, rows, :], src[f, w, rows, :])


def aligned(row):
    return row if isinstance(row, int) else pl.multiple_of(row, 8)


def advance_pair(start, middle, end, firsts, count, masked, unroll):
    steps = count // 8 + 2
    starts = [aligned(first) + (PAD - 8) for first in firsts]
    sweep(start, start, middle, MOVED, steps, starts, 1, 2, unroll, True)
    for w in range(MOVED):
        for row in masked[w]:
            rows = pl.ds(aligned(row) + PAD, 8)
            alive = start[4, w, rows, :] > 0.5
            for f in range(3):
                middle[f, w, rows, :] = jnp.where(alive, middle[f, w, rows, :], start[f, w, rows, :])
    sweep(middle, start, end, MOVED, steps, starts, 1, 2, unroll, False)


def overlay(cell, fix, board, store):
    lane = lax.broadcasted_iota(jnp.int32, (8, TILE), 1)
    for f in range(3):
        board[8 * f : 8 * f + 8, :] = fix(f)
    turned = board[...].T
    for f in range(3):
        for b in range(0, TILE, 8):
            strip = turned[b : b + 8, :]
            left = pltpu.roll(strip, (TILE - 8 * f) % TILE, 1)
            right = pltpu.roll(strip, TILE - 8 - 8 * f, 1)
            value = jnp.where(lane < REACH, left, cell(f, b))
            store(f, b, jnp.where(lane >= TILE - REACH, right, value))


def inner_kernel(lists, state, out, start, middle, end):
    lists = Lists(lists)
    _, tile = lists.outgoing()
    gather_pair(tile, lists.flags(), state, start, None)
    top = [t // CT == 0 for t in tile]
    firsts = [jnp.where(u, OUTER, 0) for u in top]
    masked = [[jnp.where(u, TILE, -8)] for u in top]
    advance_pair(start, middle, end, firsts, INNER, masked, UNROLL_INNER)
    for k in range(MOVED):
        rows = pl.ds(pl.multiple_of(firsts[k], 8) + PAD, INNER)
        for f in range(3):
            out[k, f] = end[f, k, rows, :]


def outer_kernel(lists, state, came, near, fixes, out, start, middle, end):
    lists = Lists(lists)
    _, tile = lists.outgoing()
    gather_pair(tile, lists.flags(), state, start, (came, near))
    top = [t // CT == 0 for t in tile]
    firsts = [jnp.where(u, 0, INNER) for u in top]
    masked = [[jnp.where(u, -8, TILE)] for u in top]
    advance_pair(start, middle, end, firsts, OUTER, masked, UNROLL_OUTER)
    for k in range(MOVED):
        rows = pl.ds(pl.multiple_of(firsts[k], 8) + PAD, OUTER)
        for f in range(3):
            out[k, f, 0:OUTER, :] = end[f, k, rows, :]
            out[k, f, OUTER : OUTER + 8, :] = fixes[tile[k], f]


def keep_kernel(lists, state, came, near, fixes, packed, out, start, middle, end, board, sems):
    lists = Lists(lists)
    used, tile = lists.kept()

    @pl.when(used[0])
    def _():
        gather_pair(tile, lists.flags(), state, start, (came, near))
        masked = [[-8, TILE]] * MOVED
        advance_pair(start, middle, end, [0] * MOVED, TILE, masked, UNROLL_FULL)
        board[...] = jnp.zeros_like(board)
        for k in range(MOVED):

            def store(f, b, value, k=k):
                out[k, f, b : b + 8, :] = value

            overlay(
                lambda f, b, k=k: end[f, k, PAD + b : PAD + b + 8, :],
                lambda f, k=k: fixes[tile[k], f],
                board,
                store,
            )

    out[MOVED] = jnp.zeros((3, TILE, TILE), jnp.float32)
    copies = []
    rank = jnp.int32(0)
    for s in range(SLOTS):
        entry = lists.listed[s]
        own, _ = lists.inside(entry)
        place = jnp.where(own, jnp.minimum(rank, MOVED - 1), MOVED)
        rank = rank + own.astype(jnp.int32)
        copy = pltpu.make_async_copy(out.at[place], packed.at[s], sems.at[s])
        copies.append((own | (entry < 0), copy))
    for due, copy in copies:
        pl.when(due)(copy.start)
    for due, copy in copies:
        pl.when(due)(copy.wait)


def seam_kernel(lists, turned, other, came, near, fixes, start, middle, end, one, two, side, board):
    lists = Lists(lists)
    is_left = lists.cols == 0
    flags = lists.flags()
    lane = lax.broadcasted_iota(jnp.int32, (8, TILE), 1)
    for w in range(CT):
        cols = slice(w * TILE, (w + 1) * TILE)
        for f in range(5):
            beside = other[24 + 4 * f : 28 + 4 * f, cols]
            start[f, w, PAD + 8 : PAD + 12, :] = jnp.where(is_left, beside, 0.0)
            start[f, w, PAD + 12 : PAD + 16, :] = jnp.where(is_left, 0.0, beside)
            if f < 4:
                start[f, w, PAD : PAD + 8, :] = turned[f, 0:8, cols]
                start[f, w, PAD + 16 : PAD + 40, :] = turned[f, 8:32, cols]
        for row, c in ((0, CT - 1), (16, 0), (24, 0), (32, CT - 1)):
            full = jnp.full((8, TILE), flags[w * CT + c], jnp.float32)
            start[4, w, PAD + row : PAD + row + 8, :] = full
    for f in range(5):
        for place, upper in ((0, False), (4, True)):
            rows = slice(8 * f + place, 8 * f + place + 4)
            pieces = halo_pieces(came, near, f, upper)
            one[rows, :], two[rows, :], side[rows, :] = pieces
    board[...] = jnp.zeros_like(board)
    for b in range(0, 40, 8):
        rows = slice(b, b + 8)
        first, second, beside = one[rows, :], two[rows, :], side[rows, :]
        value = jnp.where(lane < 8, pltpu.roll(second, 8, 1), 0.0)
        value = jnp.where((lane >= 8) & (lane < 12) & is_left, pltpu.roll(beside, 8, 1), value)
        far = jnp.logical_not(is_left)
        value = jnp.where((lane >= 12) & (lane < 16) & far, pltpu.roll(beside, 16, 1), value)
        value = jnp.where((lane >= 16) & (lane < 24), pltpu.roll(first, 16, 1), value)
        value = jnp.where((lane >= 24) & (lane < 32), pltpu.roll(first, 32, 1), value)
        board[rows, :] = jnp.where((lane >= 32) & (lane < 40), pltpu.roll(second, 32, 1), value)
    turned = board[...].T
    for f in range(5):
        for b in range(0, SEAM, 8):
            rows = slice(PAD + b, PAD + b + 8)
            first, second = start[f, 0, rows, :], start[f, 1, rows, :]
            ends = pltpu.roll(turned[b : b + 8, :], (8 - 8 * f) % TILE, 1)
            value = jnp.where(lane < 8, pltpu.roll(second, 8, 1), 0.0)
            value = jnp.where((lane >= 8) & (lane < 16), ends, value)
            value = jnp.where((lane >= 16) & (lane < 24), pltpu.roll(first, 16, 1), value)
            value = jnp.where((lane >= 24) & (lane < 32), pltpu.roll(first, 32, 1), value)
            start[f, CT, rows, :] = jnp.where(
                (lane >= 32) & (lane < 40), pltpu.roll(second, 32, 1), value
            )
    width = CT + 1
    sweep(start, start, middle, width, SEAM // 8, [PAD] * width, 2, 1, UNROLL_SEAM, True)
    still(middle, start, width, slice(PAD, PAD + SEAM))
    sweep(middle, start, end, width, SEAM // 8, [PAD] * width, 2, 1, UNROLL_SEAM, True)
    lane = lax.broadcasted_iota(jnp.int32, (4, TILE), 1)
    for t in range(RT * CT):
        r, c = t // CT, t % CT
        for place, row in ((0, 16 if c == 0 else 32), (4, 28 if c == 0 else 4)):
            rows = slice(PAD + row, PAD + row + 4)
            for f in range(3):
                ends = end[f, CT, rows, :]
                low = pltpu.roll(ends, 112 if r == 0 else 96, 1)
                high = pltpu.roll(ends, 96 if r == 0 else 120, 1)
                value = jnp.where(lane < REACH, low, end[f, r, rows, :])
                fixes[t, f, place : place + 4, :] = jnp.where(lane >= TILE - REACH, high, value)


def pack_kernel(lists, inner, outer, before, packed, staged, board, sems):
    del before
    lists = Lists(lists)
    board[...] = jnp.zeros_like(board)
    rank = jnp.int32(0)
    copies = []
    for s in range(SLOTS):
        entry = lists.listed[s]
        own, _ = lists.inside(entry)
        foreign = (entry >= 0) & jnp.logical_not(own)
        top = lax.rem(lax.div(jnp.maximum(entry, 0), lists.span), RT) == 0
        there = jnp.minimum(rank, MOVED - 1)
        rank = rank + foreign.astype(jnp.int32)
        parts = [
            pltpu.make_async_copy(staged.at[s, f], packed.at[s, f], sems.at[s, f]) for f in range(3)
        ]
        copies.append((foreign, parts))

        @pl.when(foreign)
        def _(s=s, there=there, top=top, parts=parts):
            def cell(f, b):
                high = jnp.where(top, b - OUTER, b)
                low = jnp.where(top, b, b - INNER)
                high = pl.multiple_of(jnp.clip(high, 0, INNER - 8), 8)
                low = pl.multiple_of(jnp.clip(low, 0, OUTER - 8), 8)
                within = jnp.where(top, b >= OUTER, b < INNER)
                if OUTER <= b < INNER:
                    return inner[there, f, pl.ds(high, 8), :]
                return jnp.where(
                    within, inner[there, f, pl.ds(high, 8), :], outer[there, f, pl.ds(low, 8), :]
                )

            def store(f, b, value):
                staged[s, f, b : b + 8, :] = value
                if b == TILE - 8:
                    parts[f].start()

            overlay(cell, lambda f: outer[there, f, OUTER : OUTER + 8, :], board, store)

    for foreign, parts in copies:

        @pl.when(foreign)
        def _(parts=parts):
            for part in parts:
                part.wait()


def passed_along(block, distance):
    count = lax.axis_size("rows")
    return lax.ppermute(block, "rows", [((i - distance) % count, i) for i in range(count)])


def swapped(block):
    return lax.ppermute(block, "cols", [(0, 1), (1, 0)])


def in_hbm(block):
    return pltpu.with_memory_space_constraint(block, pltpu.HBM)


def scratch(*shape):
    return pltpu.VMEM(shape, jnp.float32)


def shards(depth, velocity, bed, slots):
    count = lax.axis_size("rows")
    half = count // 2
    listed = slots[0, 0]
    partner = passed_along(slots, half)[0, 0]
    state, turned, again = call(
        load_kernel,
        [SMEM] + [HBM] * 3,
        [
            f32(4, CT, ROWS, TILE),
            f32(4, 32, ROWS),
            jax.ShapeDtypeStruct((SLOTS,), jnp.int32),
        ],
        [
            scratch(ROWS, COLS),
            scratch(2, ROWS, COLS),
            scratch(ROWS, COLS),
            pltpu.SemaphoreType.DMA((3,)),
        ],
    )(*[in_hbm(v) for v in (listed, depth, velocity, bed)])
    lists = jnp.concatenate([again, partner])
    own, beside = call(edge_kernel, [SMEM, VMEM, VMEM], [f32(24, COLS), f32(48, COLS)])(
        lists, state, turned
    )
    other = swapped(beside)
    (wide,) = call(wide_kernel, [VMEM, VMEM], [f32(24, 2 * COLS)])(own, other)
    route = [(2 * r, 2 * r - 1) for r in range(1, count)]
    route += [(2 * r + 1, 2 * r + 2) for r in range(count - 1)]
    came = lax.ppermute(wide, ("rows", "cols"), route)
    pair = [scratch(3, MOVED, SPAN, TILE)] * 2
    gathered = [scratch(5, MOVED, SPAN, TILE)]
    (inner,) = call(
        inner_kernel, [SMEM, VMEM], [f32(MOVED, 3, INNER, TILE)], gathered + pair
    )(lists, state)
    far_inner = passed_along(inner, half)
    near = swapped(came)
    (fixes,) = call(
        seam_kernel,
        [SMEM] + [VMEM] * 4,
        [f32(RT * CT, 3, 8, TILE)],
        [scratch(5, CT + 1, SEAM_DEEP, TILE)]
        + [scratch(3, CT + 1, SEAM_DEEP, TILE)] * 2
        + [scratch(40, TILE)] * 3
        + [scratch(TILE, TILE)],
    )(lists, turned, other, came, near)
    (outer,) = call(
        outer_kernel, [SMEM] + [VMEM] * 4, [f32(MOVED, 3, OUTER + 8, TILE)], gathered + pair
    )(lists, state, came, near, fixes)
    far_outer = passed_along(outer, half)
    place = f32(SLOTS, 3, TILE, TILE)
    (packed,) = call(
        keep_kernel,
        [SMEM] + [VMEM] * 4,
        [place],
        [scratch(MOVED + 1, 3, TILE, TILE)]
        + gathered
        + pair
        + [scratch(TILE, TILE), pltpu.SemaphoreType.DMA((SLOTS,))],
        (HBM,),
    )(lists, state, came, near, fixes)
    (packed,) = call(
        pack_kernel,
        [SMEM] + [VMEM] * 2 + [HBM],
        [place],
        [
            scratch(SLOTS, 3, TILE, TILE),
            scratch(TILE, TILE),
            pltpu.SemaphoreType.DMA((SLOTS, 3)),
        ],
        (HBM,),
        {3: 0},
    )(lists, far_inner, far_outer, packed)
    return packed[None, None]


def solution(mesh):
    in_specs = (
        P(("groups", "rows"), "cols"),
        P(None, ("groups", "rows"), "cols"),
        P(("groups", "rows"), "cols"),
        P(("groups", "rows"), "cols", None),
    )
    out_specs = P(("groups", "rows"), "cols", None, None, None, None)

    return jax.shard_map(shards, mesh=mesh, in_specs=in_specs, out_specs=out_specs, check_vma=False)
```
